512 devices in a mesh: fy: 32 (over y, x, core), fx: 16 (over z).
Axes of the slice: x: 4, y: 4, z: 16, core: 2. Of those that a mesh axis runs over, the one named last changes fastest.
Arguments:
- start_image: float32 [16, 1024, 2048], P(None, 'fy', 'fx'), may hold values from 0.2 to 2
- dirty: float32 [16, 1024, 2048], P(None, 'fy', 'fx'), may hold values from -50 to 50
- sampling: float32 [16, 1024, 2048], P(None, 'fy', 'fx'), may hold values from 0.25 to 1
- basis_seed: float32 [16, 4], replicated, may hold values from -0.75 to 2.75
- margin: int32 [32, 16, 2, 2], P('fy', 'fx'), may hold values from 8 to 30, as said below
Outputs:
- image: float32 [16, 1024, 2048], P(None, 'fy', 'fx')
- data_dual: float32 [16, 1024, 2048], P(None, 'fy', 'fx')
The draws below stay inside these ranges and needn't reach their ends.
Inputs may be any that keep to these rules, and one draw needn't show every extreme that they name: margin[a, b, l, 0] and margin[a, b, l, 1] are the widths kept above and to the left at dilation 2^l, at most 15 * 2^l; the value 30 occurs at the widest dilation in every draw.
All inputs are finite; a program needn't handle non-finite values.
Results may differ from the reference program's by a relative error of at most 0.0003.
Values sent between devices are 32-bit elements; how exact they have to be, the bound alone decides.
A program may use at most 64 MiB of HBM per device.

```python
import math
from functools import partial
import jax
import jax.numpy as jnp
from jax import lax

C = 16
RANK = 4
TAPS = 16
LEVELS = 2
ITERS = 1
ROWS_DEV = 32
COLS_DEV = 128
NROWS = 1024
NCOLS = 2048


def draw_dirty(key, part):
    first, second, third = jax.random.split(key, 3)
    row_pos = jnp.arange(NROWS).astype(jnp.float32) / NROWS
    col_pos = jnp.arange(NCOLS).astype(jnp.float32) / NCOLS
    row_scale = jnp.exp(jax.random.uniform(second, (NROWS,), jnp.float32, 0.0, math.log(3.2))) * (1.0 + row_pos)
    col_scale = jnp.exp(jax.random.uniform(third, (NCOLS,), jnp.float32, 0.0, math.log(3.2))) * (1.0 + col_pos)
    base_field = jnp.clip(jax.random.normal(first, (C, NROWS, NCOLS), jnp.float32), -4.0, 4.0)
    return 0.3 * base_field * row_scale[None, :, None] * col_scale[None, None, :]


def draw_basis_seed(key, part):
    noise = jnp.clip(jax.random.normal(key, (C, RANK), jnp.float32), -3.0, 3.0) * 0.25
    leading = (jnp.arange(C)[:, None] % RANK == jnp.arange(RANK)[None, :]).astype(jnp.float32) * 2.0
    return noise + leading


def draw_margin(key, part):
    facet_rows = NROWS // ROWS_DEV
    facet_cols = NCOLS // COLS_DEV
    reach_level = (TAPS - 1) * 2 ** jnp.arange(LEVELS)
    first, second = jax.random.split(key, 2)
    raw_cut = jax.random.randint(first, (facet_rows, facet_cols, LEVELS, 2), 0, 1 << 20)
    cut_width = raw_cut % (reach_level // 2 + 1)[None, None, :, None]
    widths = reach_level[None, None, :, None] - cut_width
    chosen = jax.random.randint(second, (), 0, facet_rows * facet_cols)
    facet_ids = jnp.arange(facet_rows * facet_cols).reshape(facet_rows, facet_cols)
    level_ids = jnp.arange(LEVELS)
    target = (facet_ids == chosen)[:, :, None, None] & (level_ids == LEVELS - 1)[None, None, :, None]
    return jnp.where(target, reach_level[LEVELS - 1], widths).astype(jnp.int32)


def block_levels(own_key, shape, shards, least, high):
    gain, own = 1.0, jax.random.fold_in(own_key, 6)
    for axis_at, parts in shards:
        draws = jnp.exp(jax.random.uniform(jax.random.fold_in(own, axis_at), (parts,), jnp.float32, least / len(shards), high / len(shards)))
        gain = gain * jnp.repeat(draws, shape[axis_at] // parts).reshape([-1 if axis == axis_at else 1 for axis in range(len(shape))])
    return gain


def setup_inputs(seed: int = 0) -> dict:
    splits = jax.random.split(jax.random.key(seed), 6)
    return {
        "start_image": jnp.clip(jnp.exp(math.log(2.0) - 2.3025851 * jax.random.uniform(splits[0], (C, NROWS, NCOLS), jnp.float32) ** block_levels(splits[0], (C, NROWS, NCOLS), ((1, 32), (2, 16)), -0.2, 0.2)), 0.2, 2.0),
        "dirty": draw_dirty(jax.random.fold_in(splits[5], 71), 0),
        "sampling": jnp.clip(0.25 + 0.75 * jax.random.uniform(splits[2], (C, NROWS, NCOLS), jnp.float32) ** block_levels(splits[2], (C, NROWS, NCOLS), ((1, 32), (2, 16)), -0.2, 0.2), 0.25, 1.0),
        "basis_seed": draw_basis_seed(jax.random.fold_in(splits[5], 71), 0),
        "margin": draw_margin(jax.random.fold_in(splits[5], 71), 0),
    }


DAUBECHIES = [-0.00011747678400228192, 0.0006754494059985568, -0.0003917403729959771, -0.00487035299301066, 0.008746094047015655, 0.013981027917015516, -0.04408825393106472, -0.01736930100202211, 0.128747426620186, 0.00047248457399797254, -0.2840155429624281, -0.015829105256023893, 0.5853546836548691, 0.6756307362980128, 0.3128715909144659, 0.05441584224308161]
DUAL_STEP = 0.5
PRIMAL_STEP = 0.5
CLIP_LEVEL = 0.08
BALL_SCALE = 0.8
NORM_EPS = 1e-06

def band_matrix(filter_taps, extent, border, dilation):
    rows_idx = jnp.arange(extent + border)[:, None]
    cols_idx = jnp.arange(extent)[None, :]
    offset = cols_idx + border - rows_idx
    matrix = jnp.zeros((extent + border, extent), jnp.float32)
    for tap_idx in range(len(filter_taps)):
        matrix = matrix + filter_taps[tap_idx] * (offset == tap_idx * dilation).astype(jnp.float32)
    return matrix

def level_tables(row_count, col_count, border, dilation):
    low_taps = [tap_value / math.sqrt(2.0) for tap_value in DAUBECHIES]
    high_taps = [(-1.0) ** tap_idx * low_taps[len(low_taps) - 1 - tap_idx] for tap_idx in range(len(low_taps))]
    return (band_matrix(low_taps, row_count, border, dilation), band_matrix(high_taps, row_count, border, dilation), band_matrix(low_taps, col_count, border, dilation), band_matrix(high_taps, col_count, border, dilation))

def facet_mask(widths_pair, row_count, col_count, border):
    row_keep = (jnp.arange(row_count + border) >= border - widths_pair[0]).astype(jnp.float32)
    col_keep = (jnp.arange(col_count + border) >= border - widths_pair[1]).astype(jnp.float32)
    return row_keep[:, None] * col_keep[None, :]

def analyse(extended, tables):
    low_rows, high_rows, low_cols, high_cols = tables
    highest = lax.Precision.HIGHEST
    col_low = jnp.einsum('cjv,vw->cjw', extended, low_cols, precision=highest)
    col_high = jnp.einsum('cjv,vw->cjw', extended, high_cols, precision=highest)
    band_lh = jnp.einsum('ji,cjw->ciw', low_rows, col_high, precision=highest)
    band_hl = jnp.einsum('ji,cjw->ciw', high_rows, col_low, precision=highest)
    band_hh = jnp.einsum('ji,cjw->ciw', high_rows, col_high, precision=highest)
    return jnp.stack([band_lh, band_hl, band_hh])

def synthesise(bands, tables):
    low_rows, high_rows, low_cols, high_cols = tables
    highest = lax.Precision.HIGHEST
    rows_high = jnp.einsum('ji,ciw->cjw', low_rows, bands[0], precision=highest) + jnp.einsum('ji,ciw->cjw', high_rows, bands[2], precision=highest)
    rows_low = jnp.einsum('ji,ciw->cjw', high_rows, bands[1], precision=highest)
    return jnp.einsum('cjw,vw->cjv', rows_high, high_cols, precision=highest) + jnp.einsum('cjw,vw->cjv', rows_low, low_cols, precision=highest)

def orthonormal(basis_seed):
    columns = []
    for column_idx in range(basis_seed.shape[1]):
        vector = basis_seed[:, column_idx]
        for previous in columns:
            vector = vector - jnp.sum(previous * vector) * previous
        vector = vector / jnp.sqrt(jnp.sum(vector * vector))
        columns.append(vector)
    return jnp.stack(columns, axis=1)

def project(spectral, stepped):
    highest = lax.Precision.HIGHEST
    weights = jnp.einsum('cr,cij->rij', spectral, stepped, precision=highest)
    return jnp.einsum('cr,rij->cij', spectral, weights, precision=highest)

def to_tiles(field, facet_rows, facet_cols):
    channels = field.shape[0]
    return field.reshape(channels, facet_rows, ROWS_DEV, facet_cols, COLS_DEV).transpose(1, 3, 0, 2, 4)

def from_tiles(tiles):
    facet_rows, facet_cols, channels, row_count, col_count = tiles.shape
    return tiles.transpose(2, 0, 3, 1, 4).reshape(channels, facet_rows * row_count, facet_cols * col_count)

def extend_whole(tiles, border):
    from_above = jnp.concatenate([jnp.zeros_like(tiles[:1, :, :, -border:, :]), tiles[:-1, :, :, -border:, :]], axis=0)
    taller = jnp.concatenate([from_above, tiles], axis=3)
    from_left = jnp.concatenate([jnp.zeros_like(taller[:, :1, :, :, -border:]), taller[:, :-1, :, :, -border:]], axis=1)
    return jnp.concatenate([from_left, taller], axis=4)

def retract_whole(grown, border):
    border_strip = grown[..., :border]
    interior = grown[..., border:]
    arrived = jnp.concatenate([border_strip[:, 1:], jnp.zeros_like(border_strip[:, :1])], axis=1)
    interior = jnp.concatenate([interior[..., :-border], interior[..., -border:] + arrived], axis=4)
    border_strip = interior[:, :, :, :border, :]
    interior = interior[:, :, :, border:, :]
    arrived = jnp.concatenate([border_strip[1:], jnp.zeros_like(border_strip[:1])], axis=0)
    return jnp.concatenate([interior[:, :, :, :-border, :], interior[:, :, :, -border:, :] + arrived], axis=3)

def reference(start_image, dirty, sampling, basis_seed, margin):
    spectral = orthonormal(basis_seed)
    facet_rows = NROWS // ROWS_DEV
    facet_cols = NCOLS // COLS_DEV
    radius = BALL_SCALE * math.sqrt(C * NROWS * NCOLS)
    weight = 1.0 / math.sqrt(LEVELS)
    current = start_image
    relaxed = start_image
    data_dual = jnp.zeros_like(start_image)
    band_duals = [jnp.zeros((facet_rows, facet_cols, 3, C, ROWS_DEV, COLS_DEV), jnp.float32) for level_idx in range(LEVELS)]
    for iteration in range(ITERS):
        shifted = data_dual + DUAL_STEP * sampling * relaxed - DUAL_STEP * dirty
        energy = jnp.sum(shifted * shifted)
        factor = jnp.maximum(0.0, 1.0 - DUAL_STEP * radius / jnp.sqrt(energy + NORM_EPS))
        data_dual = factor * shifted
        relaxed_tiles = to_tiles(relaxed, facet_rows, facet_cols)
        prior_tiles = jnp.zeros_like(relaxed_tiles)
        for level_idx in range(LEVELS):
            dilation = 2 ** level_idx
            border = (TAPS - 1) * dilation
            tables = level_tables(ROWS_DEV, COLS_DEV, border, dilation)
            keep_mask = jax.vmap(jax.vmap(partial(facet_mask, row_count=ROWS_DEV, col_count=COLS_DEV, border=border)))(margin[:, :, level_idx, :])[:, :, None]
            extended = extend_whole(relaxed_tiles, border) * keep_mask
            coefficients = jax.vmap(jax.vmap(partial(analyse, tables=tables)))(extended)
            band_duals[level_idx] = jnp.clip(band_duals[level_idx] + DUAL_STEP * weight * coefficients, -CLIP_LEVEL, CLIP_LEVEL)
            returned = jax.vmap(jax.vmap(partial(synthesise, tables=tables)))(band_duals[level_idx]) * keep_mask
            prior_tiles = prior_tiles + retract_whole(returned, border)
        stepped = current - PRIMAL_STEP * (sampling * data_dual + weight * from_tiles(prior_tiles))
        updated = jnp.maximum(project(spectral, stepped), 0.0)
        relaxed = 2.0 * updated - current
        current = updated
    return (current, data_dual)
```

```python
import math

import jax
import jax.numpy as jnp
import numpy as np
from jax import lax
from jax.experimental import pallas as pl
from jax.experimental.pallas import tpu as pltpu
from jax.sharding import PartitionSpec as P

MESH = pl.DeviceIdType.MESH
BF = jnp.bfloat16
F32 = jnp.float32

LEVELS = 2
PAD = 32
ROWS = 32
COLS = 128
CHANNELS = 16
RANK = 4
HALVES = 2
PER = CHANNELS // HALVES
GROUPS = CHANNELS // 4


DAUBECHIES = [
    -0.00011747678400228192,
    0.0006754494059985568,
    -0.0003917403729959771,
    -0.00487035299301066,
    0.008746094047015655,
    0.013981027917015516,
    -0.04408825393106472,
    -0.01736930100202211,
    0.128747426620186,
    0.00047248457399797254,
    -0.2840155429624281,
    -0.015829105256023893,
    0.5853546836548691,
    0.6756307362980128,
    0.3128715909144659,
    0.05441584224308161,
]
DUAL_STEP = 0.5
PRIMAL_STEP = 0.5
CLIP_LEVEL = 0.08
BALL_SCALE = 0.8
NORM_EPS = 1e-06


def taps_pair():
    low = [tap / math.sqrt(2.0) for tap in DAUBECHIES]
    high = [(-1.0) ** k * low[len(low) - 1 - k] for k in range(len(low))]
    return low, high


def band_matrix(taps, extent, dilation):
    matrix = np.zeros((extent + PAD, extent), np.float64)
    for k, tap in enumerate(taps):
        for i in range(extent):
            matrix[i + PAD - k * dilation, i] += tap
    return matrix


def split_host(matrix):
    high = matrix.astype(np.float32).astype(jnp.bfloat16)
    low = (matrix - high.astype(np.float64)).astype(np.float32).astype(jnp.bfloat16)
    return high, low


def tables():
    low, high = taps_pair()
    scale = DUAL_STEP / math.sqrt(LEVELS)
    rows, cols = [], []
    for level in range(LEVELS):
        d = 2**level
        rows.append(band_matrix(low, ROWS, d).T)
        rows.append(band_matrix(high, ROWS, d).T)
        both = np.concatenate([band_matrix(low, COLS, d), band_matrix(high, COLS, d)], axis=1) * scale
        cols.append(np.concatenate([both[PAD:]] + [both[:PAD]] * 4, axis=0))
    row_all = np.concatenate(rows, axis=0)
    hi, lo = (part.astype(np.float32) for part in split_host(row_all))
    forward = np.concatenate([hi, hi, lo], axis=1)
    backward = np.concatenate([hi.T, hi.T, lo.T], axis=1)
    column = []
    for level in range(LEVELS):
        column.extend(split_host(cols[level]))
    for level in range(LEVELS):
        column.extend(split_host(cols[level].T))
    return forward, backward, np.stack(column)


def split(value):
    high = value.astype(BF)
    return high, (value - high.astype(F32)).astype(BF)


def dot(a, b):
    return jnp.dot(a, b, preferred_element_type=F32)


def kernel_body(fy_count, fx_count, start_hbm, dirty_hbm, samp_hbm, basis_hbm, margin_hbm, fwd_hbm, bwd_hbm, col_hbm,
                pa_ref, pb_ref, shifted_ref, factor_ref,
                start, dirty, samp, basis, margin, fwd_raw, bwd_raw, col,
                fwd_m, bwd_m, pack, above, left_in, corner_in,
                x_own, x_left, lhs, bands, z_own, z_left, own, up_out, left_out, up_in, left_back, corner_back,
                spec, e_send, e_recv, f_send, f_recv,
                load_sem, halo_send, halo_recv, e_sem, f_sem, back_send, back_recv):
    me_y, me_x = lax.axis_index("fy"), lax.axis_index("fx")
    below, over = lax.rem(me_y + 1, fy_count), lax.rem(me_y + fy_count - 1, fy_count)
    right, left = lax.rem(me_x + 1, fx_count), lax.rem(me_x + fx_count - 1, fx_count)

    loads = []
    for at, (source, target) in enumerate([(start_hbm, start), (dirty_hbm, dirty), (samp_hbm, samp), (margin_hbm, margin),
                                           (basis_hbm, basis), (fwd_hbm, fwd_raw), (bwd_hbm, bwd_raw), (col_hbm, col)]):
        copy = pltpu.make_async_copy(source, target, load_sem.at[at])
        copy.start()
        loads.append(copy)

    barrier = pltpu.get_barrier_semaphore()

    def greet(device):
        pl.semaphore_signal(barrier, inc=1, device_id=device, device_id_type=MESH)

    def greet_x(k, carry):
        greet({"fy": me_y, "fx": lax.rem(me_x + k, fx_count)})
        return carry

    def greet_y(k, carry):
        greet({"fy": lax.rem(me_y + k, fy_count), "fx": me_x})
        return carry

    lax.fori_loop(1, fx_count, greet_x, 0)
    lax.fori_loop(1, fy_count, greet_y, 0)
    greet({"fy": below, "fx": right})
    greet({"fy": over, "fx": left})

    lane = lax.broadcasted_iota(jnp.int32, (1, COLS), 1)
    block = lane // PAD

    loads[0].wait()
    for g in range(GROUPS):
        total = jnp.zeros((ROWS, COLS), F32)
        for q in range(4):
            value = start[4 * g + q]
            moved = value if q == 3 else pltpu.roll(value, PAD * (q + 1), 1)
            total = jnp.where(block == q, moved, total)
        pack[g] = total
    loads[1].wait()
    loads[2].wait()
    energy = jnp.zeros((ROWS, COLS), F32)
    for c in range(CHANNELS):
        value = DUAL_STEP * samp[c] * start[c] - DUAL_STEP * dirty[c]
        shifted_ref[c] = value
        energy = energy + value * value
    energy = jnp.sum(energy, axis=0, keepdims=True)
    e_send[...] = energy
    e_recv[me_y] = energy

    pl.semaphore_wait(barrier, fx_count + fy_count)

    def energy_copy(k):
        return pltpu.make_async_remote_copy(
            src_ref=e_send, dst_ref=e_recv.at[me_y], send_sem=e_sem.at[0], recv_sem=e_sem.at[1],
            device_id={"fy": lax.rem(me_y + k, fy_count), "fx": me_x}, device_id_type=MESH)

    def energy_start(k, carry):
        energy_copy(k).start()
        return carry

    lax.fori_loop(1, fy_count, energy_start, 0)

    halos = []
    for h in range(HALVES):
        chans = pl.ds(h * PER, PER)
        groups = pl.ds(h * PER // 4, PER // 4)
        for at, (source, target, device) in enumerate([
            (start.at[chans], above.at[chans], {"fy": below, "fx": me_x}),
            (pack.at[groups], left_in.at[groups], {"fy": me_y, "fx": right}),
            (pack.at[groups], corner_in.at[groups], {"fy": below, "fx": right}),
        ]):
            copy = pltpu.make_async_remote_copy(
                src_ref=source, dst_ref=target, send_sem=halo_send.at[h, at], recv_sem=halo_recv.at[h, at],
                device_id=device, device_id_type=MESH)
            copy.start()
            halos.append(copy)

    for copy in loads[3:]:
        copy.wait()
    row_has = (me_y > 0).astype(jnp.int32)
    col_has = (me_x > 0).astype(jnp.int32)
    keep_rows = [margin[0, 0, l, 0] * row_has for l in range(LEVELS)]
    keep_cols = [margin[0, 0, l, 1] * col_has for l in range(LEVELS)]

    row_at = lax.broadcasted_iota(jnp.int32, (128, 192), 0)
    col_at = lax.rem(lax.broadcasted_iota(jnp.int32, (128, 192), 1), 64)
    reach = jnp.where(row_at < 64, keep_rows[0], keep_rows[1])
    fwd_m[...] = jnp.where(PAD - col_at <= reach, fwd_raw[...], 0.0).astype(BF)
    row_at = lax.broadcasted_iota(jnp.int32, (64, 384), 0)
    col_at = lax.rem(lax.broadcasted_iota(jnp.int32, (64, 384), 1), 128)
    reach = jnp.where(col_at < 64, keep_rows[0], keep_rows[1])
    bwd_m[...] = jnp.where(PAD - row_at <= reach, bwd_raw[...], 0.0).astype(BF)

    kept = []
    for l in range(LEVELS):
        inside = PAD - lax.rem(lane, PAD) <= keep_cols[l]
        kept.append([jnp.logical_and(inside, block == q) for q in range(4)])

    columns = []
    for r in range(RANK):
        vector = jnp.broadcast_to(basis[:, r : r + 1], (CHANNELS, COLS))
        for previous in columns:
            vector = vector - jnp.sum(previous * vector, axis=0, keepdims=True) * previous
        vector = vector / jnp.sqrt(jnp.sum(vector * vector, axis=0, keepdims=True))
        columns.append(vector)
        spec[r] = vector

    def project(field):
        weights = []
        for r in range(RANK):
            total = spec[r, 0:1, :] * field(0)
            for c in range(1, CHANNELS):
                total = total + spec[r, c : c + 1, :] * field(c)
            weights.append(total)

        def channel(c):
            total = spec[0, c : c + 1, :] * weights[0]
            for r in range(1, RANK):
                total = total + spec[r, c : c + 1, :] * weights[r]
            return total

        return channel

    pb = project(lambda c: PRIMAL_STEP * samp[c] * shifted_ref[c])
    for c in range(CHANNELS):
        pb_ref[c] = pb(c)

    def place(target, p, part, row0, value):
        high, low = split(value)
        lanes = pl.ds(COLS * part, COLS)
        target[p, pl.ds(row0, ROWS), lanes] = high
        target[p, pl.ds(64 + row0, ROWS), lanes] = low
        target[p, pl.ds(128 + row0, ROWS), lanes] = high

    for c in range(CHANNELS):
        place(x_own, c // 2, c % 2, PAD, start[c])

    pltpu.make_async_copy(e_recv.at[pl.ds(0, fy_count - 1)], e_recv.at[pl.ds(0, fy_count - 1)], e_sem.at[1]).wait()
    partial = jnp.sum(e_recv[...], axis=0)
    f_send[...] = partial
    f_recv[me_x] = partial

    def second_start(k, carry):
        pltpu.make_async_remote_copy(
            src_ref=f_send, dst_ref=f_recv.at[me_x], send_sem=f_sem.at[0], recv_sem=f_sem.at[1],
            device_id={"fy": me_y, "fx": lax.rem(me_x + k, fx_count)}, device_id_type=MESH).start()
        return carry

    lax.fori_loop(1, fx_count, second_start, 0)

    backs = []
    for h in range(HALVES):
        for copy in halos[3 * h : 3 * h + 3]:
            copy.wait_recv()
        first = h * PER
        for c in range(first, first + PER):
            place(x_own, c // 2, c % 2, 0, above[c])
        for g in range(first // 4, (first + PER) // 4):
            place(x_left, g // 2, g % 2, 0, corner_in[g])
            place(x_left, g // 2, g % 2, PAD, left_in[g])
        for p in range(first // 2, (first + PER) // 2):
            u = dot(fwd_m[...], x_own[p])
            high, low = split(u)
            for part in range(2):
                c = 2 * p + part - first
                lanes = slice(COLS * part, COLS * (part + 1))
                for l in range(LEVELS):
                    lhs[l, pl.ds(64 * c, 64), 0:128] = high[64 * l : 64 * l + 64, lanes]
                    lhs[l, pl.ds(64 * c, 64), 256:384] = low[64 * l : 64 * l + 64, lanes]
        for p in range(first // 8, (first + PER) // 8):
            u = dot(fwd_m[...], x_left[p])
            for part in range(2):
                for q in range(4):
                    c = 8 * p + 4 * part + q - first
                    for l in range(LEVELS):
                        value = jnp.where(kept[l][q], u[64 * l : 64 * l + 64, COLS * part : COLS * (part + 1)], 0.0)
                        high, low = split(value)
                        lhs[l, pl.ds(64 * c, 64), 128:256] = high
                        lhs[l, pl.ds(64 * c, 64), 384:512] = low
        z_sum = [[jnp.zeros((64, COLS), F32) for l in range(LEVELS)] for g in range(PER // 4)]
        for l in range(LEVELS):
            acc = dot(lhs[l, :, 0:256], col[2 * l]) + dot(lhs[l, :, 256:512], col[2 * l]) + dot(lhs[l, :, 0:256], col[2 * l + 1])
            acc = jnp.clip(acc, -CLIP_LEVEL, CLIP_LEVEL)
            high, low = split(acc)
            for c in range(PER):
                zero = jnp.zeros((32, COLS), BF)
                top, mid, end = 64 * c, 64 * c + 32, 64 * c + 64
                bands[pl.ds(top, 32), 0:128] = zero
                bands[pl.ds(top, 32), 256:384] = zero
                bands[pl.ds(top, 32), 128:256] = high[top:mid, 128:256]
                bands[pl.ds(top, 32), 384:512] = low[top:mid, 128:256]
                bands[pl.ds(mid, 32), 0:256] = high[mid:end, :]
                bands[pl.ds(mid, 32), 256:512] = low[mid:end, :]
            at = 2 * LEVELS + 2 * l
            z = dot(bands[:, 0:256], col[at]) + dot(bands[:, 256:512], col[at]) + dot(bands[:, 0:256], col[at + 1])
            for c in range(PER):
                high, low = split(z[64 * c : 64 * c + 64, 0:128])
                lanes = pl.ds(COLS * (c % 2), COLS)
                z_own[c // 2, pl.ds(64 * l, 64), lanes] = high
                z_own[c // 2, pl.ds(128 + 64 * l, 64), lanes] = low
                piece = z[64 * c : 64 * c + 64, 128:256]
                z_sum[c // 4][l] = z_sum[c // 4][l] + jnp.where(kept[l][c % 4], piece, 0.0)
        for g in range(PER // 4):
            lanes = pl.ds(COLS * (g % 2), COLS)
            for l in range(LEVELS):
                high, low = split(z_sum[g][l])
                z_left[g // 2, pl.ds(64 * l, 64), lanes] = high
                z_left[g // 2, pl.ds(128 + 64 * l, 64), lanes] = low
        for p in range(PER // 8):
            r = dot(bwd_m[:, 0:256], z_left[p]) + dot(bwd_m[:, 256:384], z_left[p, 0:128, :])
            for part in range(2):
                left_out[first // 4 + 2 * p + part] = r[:, COLS * part : COLS * (part + 1)]
        for p in range(PER // 2):
            r = dot(bwd_m[:, 0:256], z_own[p]) + dot(bwd_m[:, 256:384], z_own[p, 0:128, :])
            for part in range(2):
                c = first + 2 * p + part
                up_out[c] = r[0:32, COLS * part : COLS * (part + 1)]
                own[c] = r[32:64, COLS * part : COLS * (part + 1)]
        chans = pl.ds(first, PER)
        groups = pl.ds(first // 4, PER // 4)
        for at, (source, target, device) in enumerate([
            (left_out.at[groups, pl.ds(32, 32), :], left_back.at[groups], {"fy": me_y, "fx": left}),
            (left_out.at[groups, pl.ds(0, 32), :], corner_back.at[groups], {"fy": over, "fx": left}),
            (up_out.at[chans], up_in.at[chans], {"fy": over, "fx": me_x}),
        ]):
            copy = pltpu.make_async_remote_copy(
                src_ref=source, dst_ref=target, send_sem=back_send.at[h, at], recv_sem=back_recv.at[h, at],
                device_id=device, device_id_type=MESH)
            copy.start()
            backs.append(copy)

    for copy in backs:
        copy.wait_recv()
    for g in range(GROUPS):
        strip = left_back[g] + corner_back[g]
        for q in range(4):
            c = 4 * g + q
            moved = strip if q == 3 else pltpu.roll(strip, COLS - PAD * (q + 1), 1)
            own[c] = start[c] - (own[c] + up_in[c] + jnp.where(block == 3, moved, 0.0))
    pa = project(lambda c: own[c])
    for c in range(CHANNELS):
        pa_ref[c] = pa(c)

    pltpu.make_async_copy(f_recv.at[pl.ds(0, fx_count - 1)], f_recv.at[pl.ds(0, fx_count - 1)], f_sem.at[1]).wait()
    total = jnp.sum(jnp.sum(f_recv[...], axis=0), axis=1, keepdims=True)
    radius = BALL_SCALE * math.sqrt(CHANNELS * ROWS * COLS * fy_count * fx_count)
    factor = jnp.maximum(0.0, 1.0 - DUAL_STEP * radius / jnp.sqrt(total + NORM_EPS))
    factor_ref[...] = jnp.broadcast_to(factor, (1, COLS))

    for copy in halos + backs:
        copy.wait_send()
    pltpu.make_async_copy(e_recv.at[pl.ds(0, fy_count - 1)], e_recv.at[pl.ds(0, fy_count - 1)], e_sem.at[0]).wait()
    pltpu.make_async_copy(f_recv.at[pl.ds(0, fx_count - 1)], f_recv.at[pl.ds(0, fx_count - 1)], f_sem.at[0]).wait()


def per_device(fy_count, fx_count, start_image, dirty, sampling, basis_seed, margin):
    forward, backward, column = tables()
    tile = jax.ShapeDtypeStruct((CHANNELS, ROWS, COLS), F32)
    hbm = pl.BlockSpec(memory_space=pltpu.HBM)
    vmem = pl.BlockSpec(memory_space=pltpu.VMEM)
    field = pltpu.VMEM((CHANNELS, ROWS, COLS), F32)
    strips = pltpu.VMEM((GROUPS, ROWS, COLS), F32)
    dma = pltpu.SemaphoreType.DMA

    def body(*refs):
        kernel_body(fy_count, fx_count, *refs)

    pa, pb, shifted, factor = pl.pallas_call(
        body,
        out_shape=(tile, tile, tile, jax.ShapeDtypeStruct((1, COLS), F32)),
        in_specs=[hbm] * 8,
        out_specs=(vmem,) * 4,
        scratch_shapes=[
            field, field, field,
            pltpu.VMEM((CHANNELS, RANK), F32),
            pltpu.SMEM((1, 1, LEVELS, 2), jnp.int32),
            pltpu.VMEM((128, 192), F32), pltpu.VMEM((64, 384), F32), pltpu.VMEM((4 * LEVELS, 256, 256), BF),
            pltpu.VMEM((128, 192), BF), pltpu.VMEM((64, 384), BF),
            strips, field, strips, strips,
            pltpu.VMEM((CHANNELS // 2, 192, 256), BF), pltpu.VMEM((GROUPS // 2, 192, 256), BF),
            pltpu.VMEM((LEVELS, 64 * PER, 512), BF), pltpu.VMEM((64 * PER, 512), BF),
            pltpu.VMEM((PER // 2, 256, 256), BF), pltpu.VMEM((PER // 8, 256, 256), BF),
            field, field, pltpu.VMEM((GROUPS, 64, COLS), F32), field, strips, strips,
            pltpu.VMEM((RANK, CHANNELS, COLS), F32),
            pltpu.VMEM((1, COLS), F32), pltpu.VMEM((fy_count, 1, COLS), F32),
            pltpu.VMEM((1, COLS), F32), pltpu.VMEM((fx_count, 1, COLS), F32),
            dma((8,)), dma((HALVES, 3)), dma((HALVES, 3)), dma((2,)), dma((2,)), dma((HALVES, 3)), dma((HALVES, 3)),
        ],
        compiler_params=pltpu.CompilerParams(collective_id=0, has_side_effects=True, vmem_limit_bytes=40 * 1024 * 1024),
        name="step",
    )(start_image, dirty, sampling, basis_seed, margin,
      jnp.asarray(forward, F32), jnp.asarray(backward, F32), jnp.asarray(column, BF))
    factor = factor[0, 0]
    return jnp.maximum(pa - factor * pb, 0.0), factor * shifted


def solution(mesh):
    fy_count, fx_count = mesh.shape["fy"], mesh.shape["fx"]

    def step(*args):
        return per_device(fy_count, fx_count, *args)

    image = P(None, "fy", "fx")
    return jax.shard_map(
        step, mesh=mesh, in_specs=(image, image, image, P(), P("fy", "fx", None, None)),
        out_specs=(image, image), check_vma=False)
```

```python
import math

import jax
import jax.numpy as jnp
import numpy as np
from jax import lax
from jax.experimental import pallas as pl
from jax.experimental.pallas import tpu as pltpu
from jax.sharding import PartitionSpec as P

MESH = pl.DeviceIdType.MESH
BF = jnp.bfloat16
F32 = jnp.float32

LEVELS = 2
PAD = 32
ROWS = 32
COLS = 128
CHANNELS = 16
RANK = 4
HALVES = 2
PER = CHANNELS // HALVES
GROUPS = CHANNELS // 4


DAUBECHIES = [
    -0.00011747678400228192,
    0.0006754494059985568,
    -0.0003917403729959771,
    -0.00487035299301066,
    0.008746094047015655,
    0.013981027917015516,
    -0.04408825393106472,
    -0.01736930100202211,
    0.128747426620186,
    0.00047248457399797254,
    -0.2840155429624281,
    -0.015829105256023893,
    0.5853546836548691,
    0.6756307362980128,
    0.3128715909144659,
    0.05441584224308161,
]
DUAL_STEP = 0.5
PRIMAL_STEP = 0.5
CLIP_LEVEL = 0.08
BALL_SCALE = 0.8
NORM_EPS = 1e-06


def taps_pair():
    low = [tap / math.sqrt(2.0) for tap in DAUBECHIES]
    high = [(-1.0) ** k * low[len(low) - 1 - k] for k in range(len(low))]
    return low, high


def band_matrix(taps, extent, dilation):
    matrix = np.zeros((extent + PAD, extent), np.float64)
    for k, tap in enumerate(taps):
        for i in range(extent):
            matrix[i + PAD - k * dilation, i] += tap
    return matrix


def split_host(matrix):
    high = matrix.astype(np.float32).astype(jnp.bfloat16)
    low = (matrix - high.astype(np.float64)).astype(np.float32).astype(jnp.bfloat16)
    return high, low


def tables():
    low, high = taps_pair()
    scale = DUAL_STEP / math.sqrt(LEVELS)
    rows, cols = [], []
    for level in range(LEVELS):
        d = 2**level
        rows.append(band_matrix(low, ROWS, d).T)
        rows.append(band_matrix(high, ROWS, d).T)
        both = np.concatenate([band_matrix(low, COLS, d), band_matrix(high, COLS, d)], axis=1) * scale
        cols.append(np.concatenate([both[PAD:]] + [both[:PAD]] * 4, axis=0))
    row_all = np.concatenate(rows, axis=0)
    hi, lo = (part.astype(np.float32) for part in split_host(row_all))
    forward = np.concatenate([hi, hi, lo], axis=1)
    backward = np.concatenate([hi.T, hi.T, lo.T], axis=1)
    column = []
    for level in range(LEVELS):
        column.extend(split_host(cols[level]))
    for level in range(LEVELS):
        column.extend(split_host(cols[level].T))
    return forward, backward, np.stack(column)


def split(value):
    high = value.astype(BF)
    return high, (value - high.astype(F32)).astype(BF)


def dot(a, b):
    return jnp.dot(a, b, preferred_element_type=F32)


def kernel_body(fy_count, fx_count, start_hbm, dirty_hbm, samp_hbm, basis_hbm, margin_hbm, fwd_hbm, bwd_hbm, col_hbm,
                pa_ref, pb_ref, shifted_ref, factor_ref,
                start, dirty, samp, basis, margin, fwd_raw, bwd_raw, col,
                fwd_m, bwd_m, pack, above, left_in, corner_in,
                x_own, x_left, lhs, bands, z_own, z_left, own, up_out, left_out, up_in, left_back, corner_back,
                spec, e_send, e_recv, f_send, f_recv,
                load_sem, halo_send, halo_recv, e_sem, f_sem, back_send, back_recv, far_sem):
    me_y, me_x = lax.axis_index("fy"), lax.axis_index("fx")
    below, over = lax.rem(me_y + 1, fy_count), lax.rem(me_y + fy_count - 1, fy_count)
    right, left = lax.rem(me_x + 1, fx_count), lax.rem(me_x + fx_count - 1, fx_count)

    loads = []
    for at, (source, target) in enumerate([(start_hbm, start), (dirty_hbm, dirty), (samp_hbm, samp), (margin_hbm, margin),
                                           (basis_hbm, basis), (fwd_hbm, fwd_raw), (bwd_hbm, bwd_raw), (col_hbm, col)]):
        copy = pltpu.make_async_copy(source, target, load_sem.at[at])
        copy.start()
        loads.append(copy)

    barrier = pltpu.get_barrier_semaphore()

    def greet(device):
        pl.semaphore_signal(barrier, inc=1, device_id=device, device_id_type=MESH)

    def greet_x(k, carry):
        greet({"fy": me_y, "fx": lax.rem(me_x + k, fx_count)})
        return carry

    def greet_y(k, carry):
        greet({"fy": lax.rem(me_y + k, fy_count), "fx": me_x})
        return carry

    near = fx_count // 4
    lax.fori_loop(1, fy_count, greet_y, 0)
    lax.fori_loop(1, near + 1, greet_x, 0)
    lax.fori_loop(fx_count - near, fx_count, greet_x, 0)
    greet({"fy": below, "fx": right})
    greet({"fy": over, "fx": left})

    lane = lax.broadcasted_iota(jnp.int32, (1, COLS), 1)
    block = lane // PAD

    loads[0].wait()
    for g in range(GROUPS):
        total = jnp.zeros((ROWS, COLS), F32)
        for q in range(4):
            value = start[4 * g + q]
            moved = value if q == 3 else pltpu.roll(value, PAD * (q + 1), 1)
            total = jnp.where(block == q, moved, total)
        pack[g] = total
    loads[1].wait()
    loads[2].wait()
    energy = jnp.zeros((ROWS, COLS), F32)
    for c in range(CHANNELS):
        value = DUAL_STEP * samp[c] * start[c] - DUAL_STEP * dirty[c]
        shifted_ref[c] = value
        energy = energy + value * value
    energy = jnp.sum(energy, axis=0, keepdims=True)
    e_send[...] = energy
    e_recv[me_y] = energy

    pl.semaphore_wait(barrier, fy_count - 1 + 2 * near + 2)
    for device in (near, fx_count - near):
        pl.semaphore_signal(far_sem, inc=1, device_id={"fy": me_y, "fx": lax.rem(me_x + device, fx_count)}, device_id_type=MESH)

    def energy_copy(k):
        return pltpu.make_async_remote_copy(
            src_ref=e_send, dst_ref=e_recv.at[me_y], send_sem=e_sem.at[0], recv_sem=e_sem.at[1],
            device_id={"fy": lax.rem(me_y + k, fy_count), "fx": me_x}, device_id_type=MESH)

    def energy_start(k, carry):
        energy_copy(k).start()
        return carry

    lax.fori_loop(1, fy_count, energy_start, 0)

    halos = []
    for h in range(HALVES):
        chans = pl.ds(h * PER, PER)
        groups = pl.ds(h * PER // 4, PER // 4)
        for at, (source, target, device) in enumerate([
            (start.at[chans], above.at[chans], {"fy": below, "fx": me_x}),
            (pack.at[groups], left_in.at[groups], {"fy": me_y, "fx": right}),
            (pack.at[groups], corner_in.at[groups], {"fy": below, "fx": right}),
        ]):
            copy = pltpu.make_async_remote_copy(
                src_ref=source, dst_ref=target, send_sem=halo_send.at[h, at], recv_sem=halo_recv.at[h, at],
                device_id=device, device_id_type=MESH)
            copy.start()
            halos.append(copy)

    for copy in loads[3:]:
        copy.wait()
    row_has = (me_y > 0).astype(jnp.int32)
    col_has = (me_x > 0).astype(jnp.int32)
    keep_rows = [margin[0, 0, l, 0] * row_has for l in range(LEVELS)]
    keep_cols = [margin[0, 0, l, 1] * col_has for l in range(LEVELS)]

    row_at = lax.broadcasted_iota(jnp.int32, (128, 192), 0)
    col_at = lax.rem(lax.broadcasted_iota(jnp.int32, (128, 192), 1), 64)
    reach = jnp.where(row_at < 64, keep_rows[0], keep_rows[1])
    fwd_m[...] = jnp.where(PAD - col_at <= reach, fwd_raw[...], 0.0).astype(BF)
    row_at = lax.broadcasted_iota(jnp.int32, (64, 384), 0)
    col_at = lax.rem(lax.broadcasted_iota(jnp.int32, (64, 384), 1), 128)
    reach = jnp.where(col_at < 64, keep_rows[0], keep_rows[1])
    bwd_m[...] = jnp.where(PAD - row_at <= reach, bwd_raw[...], 0.0).astype(BF)

    kept = []
    for l in range(LEVELS):
        inside = PAD - lax.rem(lane, PAD) <= keep_cols[l]
        kept.append([jnp.logical_and(inside, block == q) for q in range(4)])

    columns = []
    diagonal = lax.broadcasted_iota(jnp.int32, (CHANNELS, CHANNELS), 0) == lax.broadcasted_iota(jnp.int32, (CHANNELS, CHANNELS), 1)
    for r in range(RANK):
        vector = jnp.sum(jnp.where(diagonal, basis[r : r + 1, :], 0.0), axis=1, keepdims=True)
        vector = jnp.broadcast_to(vector, (CHANNELS, COLS))
        for previous in columns:
            vector = vector - jnp.sum(previous * vector, axis=0, keepdims=True) * previous
        vector = vector / jnp.sqrt(jnp.sum(vector * vector, axis=0, keepdims=True))
        columns.append(vector)
        spec[r] = vector

    def project(field):
        weights = []
        for r in range(RANK):
            total = spec[r, 0:1, :] * field(0)
            for c in range(1, CHANNELS):
                total = total + spec[r, c : c + 1, :] * field(c)
            weights.append(total)

        def channel(c):
            total = spec[0, c : c + 1, :] * weights[0]
            for r in range(1, RANK):
                total = total + spec[r, c : c + 1, :] * weights[r]
            return total

        return channel

    pb = project(lambda c: PRIMAL_STEP * samp[c] * shifted_ref[c])
    for c in range(CHANNELS):
        pb_ref[c] = pb(c)

    def place(target, p, part, row0, value):
        high, low = split(value)
        lanes = pl.ds(COLS * part, COLS)
        target[p, pl.ds(row0, ROWS), lanes] = high
        target[p, pl.ds(64 + row0, ROWS), lanes] = low
        target[p, pl.ds(128 + row0, ROWS), lanes] = high

    for c in range(CHANNELS):
        place(x_own, c // 2, c % 2, PAD, start[c])

    pltpu.make_async_copy(e_recv.at[pl.ds(0, fy_count - 1)], e_recv.at[pl.ds(0, fy_count - 1)], e_sem.at[1]).wait()
    partial = jnp.sum(e_recv[...], axis=0)
    f_send[...] = partial
    f_recv[me_x] = partial

    pl.semaphore_wait(far_sem, 2)

    def second_start(k, carry):
        pltpu.make_async_remote_copy(
            src_ref=f_send, dst_ref=f_recv.at[me_x], send_sem=f_sem.at[0], recv_sem=f_sem.at[1],
            device_id={"fy": me_y, "fx": lax.rem(me_x + k, fx_count)}, device_id_type=MESH).start()
        return carry

    lax.fori_loop(1, fx_count, second_start, 0)

    backs = []
    for h in range(HALVES):
        for copy in halos[3 * h : 3 * h + 3]:
            copy.wait_recv()
        first = h * PER
        for c in range(first, first + PER):
            place(x_own, c // 2, c % 2, 0, above[c])
        for g in range(first // 4, (first + PER) // 4):
            place(x_left, g // 2, g % 2, 0, corner_in[g])
            place(x_left, g // 2, g % 2, PAD, left_in[g])
        for p in range(first // 2, (first + PER) // 2):
            u = dot(fwd_m[...], x_own[p])
            high, low = split(u)
            for part in range(2):
                c = 2 * p + part - first
                lanes = slice(COLS * part, COLS * (part + 1))
                for l in range(LEVELS):
                    lhs[l, pl.ds(64 * c, 64), 0:128] = high[64 * l : 64 * l + 64, lanes]
                    lhs[l, pl.ds(64 * c, 64), 256:384] = low[64 * l : 64 * l + 64, lanes]
        for p in range(first // 8, (first + PER) // 8):
            u = dot(fwd_m[...], x_left[p])
            for part in range(2):
                for q in range(4):
                    c = 8 * p + 4 * part + q - first
                    for l in range(LEVELS):
                        value = jnp.where(kept[l][q], u[64 * l : 64 * l + 64, COLS * part : COLS * (part + 1)], 0.0)
                        high, low = split(value)
                        lhs[l, pl.ds(64 * c, 64), 128:256] = high
                        lhs[l, pl.ds(64 * c, 64), 384:512] = low
        z_sum = [[jnp.zeros((64, COLS), F32) for l in range(LEVELS)] for g in range(PER // 4)]
        for l in range(LEVELS):
            acc = dot(lhs[l, :, 0:256], col[2 * l]) + dot(lhs[l, :, 256:512], col[2 * l]) + dot(lhs[l, :, 0:256], col[2 * l + 1])
            acc = jnp.clip(acc, -CLIP_LEVEL, CLIP_LEVEL)
            high, low = split(acc)
            for c in range(PER):
                zero = jnp.zeros((32, COLS), BF)
                top, mid, end = 64 * c, 64 * c + 32, 64 * c + 64
                bands[pl.ds(top, 32), 0:128] = zero
                bands[pl.ds(top, 32), 256:384] = zero
                bands[pl.ds(top, 32), 128:256] = high[top:mid, 128:256]
                bands[pl.ds(top, 32), 384:512] = low[top:mid, 128:256]
                bands[pl.ds(mid, 32), 0:256] = high[mid:end, :]
                bands[pl.ds(mid, 32), 256:512] = low[mid:end, :]
            at = 2 * LEVELS + 2 * l
            z = dot(bands[:, 0:256], col[at]) + dot(bands[:, 256:512], col[at]) + dot(bands[:, 0:256], col[at + 1])
            for c in range(PER):
                high, low = split(z[64 * c : 64 * c + 64, 0:128])
                lanes = pl.ds(COLS * (c % 2), COLS)
                z_own[c // 2, pl.ds(64 * l, 64), lanes] = high
                z_own[c // 2, pl.ds(128 + 64 * l, 64), lanes] = low
                piece = z[64 * c : 64 * c + 64, 128:256]
                z_sum[c // 4][l] = z_sum[c // 4][l] + jnp.where(kept[l][c % 4], piece, 0.0)
        for g in range(PER // 4):
            lanes = pl.ds(COLS * (g % 2), COLS)
            for l in range(LEVELS):
                high, low = split(z_sum[g][l])
                z_left[g // 2, pl.ds(64 * l, 64), lanes] = high
                z_left[g // 2, pl.ds(128 + 64 * l, 64), lanes] = low
        for p in range(PER // 8):
            r = dot(bwd_m[:, 0:256], z_left[p]) + dot(bwd_m[:, 256:384], z_left[p, 0:128, :])
            for part in range(2):
                left_out[first // 4 + 2 * p + part] = r[:, COLS * part : COLS * (part + 1)]
        for p in range(PER // 2):
            r = dot(bwd_m[:, 0:256], z_own[p]) + dot(bwd_m[:, 256:384], z_own[p, 0:128, :])
            for part in range(2):
                c = first + 2 * p + part
                up_out[c] = r[0:32, COLS * part : COLS * (part + 1)]
                own[c] = r[32:64, COLS * part : COLS * (part + 1)]
        chans = pl.ds(first, PER)
        groups = pl.ds(first // 4, PER // 4)
        for at, (source, target, device) in enumerate([
            (left_out.at[groups, pl.ds(32, 32), :], left_back.at[groups], {"fy": me_y, "fx": left}),
            (left_out.at[groups, pl.ds(0, 32), :], corner_back.at[groups], {"fy": over, "fx": left}),
            (up_out.at[chans], up_in.at[chans], {"fy": over, "fx": me_x}),
        ]):
            copy = pltpu.make_async_remote_copy(
                src_ref=source, dst_ref=target, send_sem=back_send.at[h, at], recv_sem=back_recv.at[h, at],
                device_id=device, device_id_type=MESH)
            copy.start()
            backs.append(copy)

    for copy in backs:
        copy.wait_recv()
    for g in range(GROUPS):
        strip = left_back[g] + corner_back[g]
        for q in range(4):
            c = 4 * g + q
            moved = strip if q == 3 else pltpu.roll(strip, COLS - PAD * (q + 1), 1)
            own[c] = start[c] - (own[c] + up_in[c] + jnp.where(block == 3, moved, 0.0))
    pa = project(lambda c: own[c])
    for c in range(CHANNELS):
        pa_ref[c] = pa(c)

    pltpu.make_async_copy(f_recv.at[pl.ds(0, fx_count - 1)], f_recv.at[pl.ds(0, fx_count - 1)], f_sem.at[1]).wait()
    total = jnp.sum(jnp.sum(f_recv[...], axis=0), axis=1, keepdims=True)
    radius = BALL_SCALE * math.sqrt(CHANNELS * ROWS * COLS * fy_count * fx_count)
    factor = jnp.maximum(0.0, 1.0 - DUAL_STEP * radius / jnp.sqrt(total + NORM_EPS))
    factor_ref[...] = jnp.broadcast_to(factor, (1, COLS))

    for copy in halos + backs:
        copy.wait_send()
    pltpu.make_async_copy(e_recv.at[pl.ds(0, fy_count - 1)], e_recv.at[pl.ds(0, fy_count - 1)], e_sem.at[0]).wait()
    pltpu.make_async_copy(f_recv.at[pl.ds(0, fx_count - 1)], f_recv.at[pl.ds(0, fx_count - 1)], f_sem.at[0]).wait()


def per_device(fy_count, fx_count, start_image, dirty, sampling, basis_seed, margin):
    forward, backward, column = tables()
    tile = jax.ShapeDtypeStruct((CHANNELS, ROWS, COLS), F32)
    hbm = pl.BlockSpec(memory_space=pltpu.HBM)
    vmem = pl.BlockSpec(memory_space=pltpu.VMEM)
    field = pltpu.VMEM((CHANNELS, ROWS, COLS), F32)
    strips = pltpu.VMEM((GROUPS, ROWS, COLS), F32)
    dma = pltpu.SemaphoreType.DMA

    def body(*refs):
        kernel_body(fy_count, fx_count, *refs)

    pa, pb, shifted, factor = pl.pallas_call(
        body,
        out_shape=(tile, tile, tile, jax.ShapeDtypeStruct((1, COLS), F32)),
        in_specs=[hbm] * 8,
        out_specs=(vmem,) * 4,
        scratch_shapes=[
            field, field, field,
            pltpu.VMEM((RANK, CHANNELS), F32),
            pltpu.SMEM((1, 1, LEVELS, 2), jnp.int32),
            pltpu.VMEM((128, 192), F32), pltpu.VMEM((64, 384), F32), pltpu.VMEM((4 * LEVELS, 256, 256), BF),
            pltpu.VMEM((128, 192), BF), pltpu.VMEM((64, 384), BF),
            strips, field, strips, strips,
            pltpu.VMEM((CHANNELS // 2, 192, 256), BF), pltpu.VMEM((GROUPS // 2, 192, 256), BF),
            pltpu.VMEM((LEVELS, 64 * PER, 512), BF), pltpu.VMEM((64 * PER, 512), BF),
            pltpu.VMEM((PER // 2, 256, 256), BF), pltpu.VMEM((PER // 8, 256, 256), BF),
            field, field, pltpu.VMEM((GROUPS, 64, COLS), F32), field, strips, strips,
            pltpu.VMEM((RANK, CHANNELS, COLS), F32),
            pltpu.VMEM((1, COLS), F32), pltpu.VMEM((fy_count, 1, COLS), F32),
            pltpu.VMEM((1, COLS), F32), pltpu.VMEM((fx_count, 1, COLS), F32),
            dma((8,)), dma((HALVES, 3)), dma((HALVES, 3)), dma((2,)), dma((2,)), dma((HALVES, 3)), dma((HALVES, 3)),
            pltpu.SemaphoreType.REGULAR,
        ],
        compiler_params=pltpu.CompilerParams(collective_id=0, has_side_effects=True, vmem_limit_bytes=40 * 1024 * 1024),
        name="step",
    )(*(pltpu.with_memory_space_constraint(value, pltpu.HBM) for value in (
        start_image, dirty, sampling, basis_seed.T, margin,
        jnp.asarray(forward, F32), jnp.asarray(backward, F32), jnp.asarray(column, BF))))
    factor = factor[0, 0]
    return jnp.maximum(pa - factor * pb, 0.0), factor * shifted


def solution(mesh):
    fy_count, fx_count = mesh.shape["fy"], mesh.shape["fx"]

    def step(*args):
        return per_device(fy_count, fx_count, *args)

    image = P(None, "fy", "fx")
    return jax.shard_map(
        step, mesh=mesh, in_specs=(image, image, image, P(), P("fy", "fx", None, None)),
        out_specs=(image, image), check_vma=False)
```

```python
import functools
import math

import jax
import jax.numpy as jnp
import numpy as np
from jax import lax
from jax.experimental import pallas as pl
from jax.experimental.pallas import tpu as pltpu
from jax.sharding import PartitionSpec as P

MESH = pl.DeviceIdType.MESH
BF = jnp.bfloat16
F32 = jnp.float32

LEVELS = 2
PAD = 32
ROWS = 32
COLS = 128
CHANNELS = 16
RANK = 4
HALVES = 2
EARLY = 4
PER = CHANNELS // HALVES
GROUPS = CHANNELS // 4


DAUBECHIES = [
    -0.00011747678400228192,
    0.0006754494059985568,
    -0.0003917403729959771,
    -0.00487035299301066,
    0.008746094047015655,
    0.013981027917015516,
    -0.04408825393106472,
    -0.01736930100202211,
    0.128747426620186,
    0.00047248457399797254,
    -0.2840155429624281,
    -0.015829105256023893,
    0.5853546836548691,
    0.6756307362980128,
    0.3128715909144659,
    0.05441584224308161,
]
DUAL_STEP = 0.5
PRIMAL_STEP = 0.5
CLIP_LEVEL = 0.08
BALL_SCALE = 0.8
NORM_EPS = 1e-06


def taps_pair():
    low = [tap / math.sqrt(2.0) for tap in DAUBECHIES]
    high = [(-1.0) ** k * low[len(low) - 1 - k] for k in range(len(low))]
    return low, high


def band_matrix(taps, extent, dilation):
    matrix = np.zeros((extent + PAD, extent), np.float64)
    for k, tap in enumerate(taps):
        for i in range(extent):
            matrix[i + PAD - k * dilation, i] += tap
    return matrix


def split_host(matrix):
    high = matrix.astype(np.float32).astype(jnp.bfloat16)
    low = (matrix - high.astype(np.float64)).astype(np.float32).astype(jnp.bfloat16)
    return high, low


def tables():
    low, high = taps_pair()
    scale = DUAL_STEP / math.sqrt(LEVELS)
    rows, cols = [], []
    for level in range(LEVELS):
        d = 2**level
        rows.append(band_matrix(low, ROWS, d).T)
        rows.append(band_matrix(high, ROWS, d).T)
        both = np.concatenate([band_matrix(low, COLS, d), band_matrix(high, COLS, d)], axis=1) * scale
        cols.append(np.concatenate([both[PAD:]] + [both[:PAD]] * 4, axis=0))
    row_all = np.concatenate(rows, axis=0)
    hi, lo = (part.astype(np.float32) for part in split_host(row_all))
    forward = np.concatenate([hi, hi, lo], axis=1)
    backward = np.concatenate([hi.T, hi.T, lo.T], axis=1)
    column = []
    for level in range(LEVELS):
        column.append(split_host(cols[level])[0])
    for level in range(LEVELS):
        column.append(split_host(cols[level].T)[0])
    return forward, backward, np.stack(column)


def split(value):
    high = value.astype(BF)
    return high, (value - high.astype(F32)).astype(BF)


def dot(a, b):
    return jnp.dot(a, b, preferred_element_type=F32)


def kernel_body(fy_count, fx_count, start_hbm, dirty_hbm, samp_hbm, basis_hbm, margin_hbm, fwd_hbm, bwd_hbm, col_hbm,
                pa_ref, pb_ref, shifted_ref, factor_ref,
                start, dirty, samp, basis, margin, fwd_raw, bwd_raw, col,
                fwd_m, bwd_m, pack, above, left_in, corner_in,
                x_own, x_left, lhs, bands, z_own, z_left, own, up_out, left_out, up_in, left_back, corner_back,
                spec, line_out, line_in, plane_out, plane_in, total_out, total_in,
                load_sem, halo_send, halo_recv, line_sem, plane_sem, total_sem, back_send, back_recv):
    me_y, me_x = lax.axis_index("fy"), lax.axis_index("fx")
    below, over = lax.rem(me_y + 1, fy_count), lax.rem(me_y + fy_count - 1, fy_count)
    right, left = lax.rem(me_x + 1, fx_count), lax.rem(me_x + fx_count - 1, fx_count)

    loads = []
    for at, (source, target) in enumerate([(start_hbm, start), (dirty_hbm, dirty), (samp_hbm, samp), (margin_hbm, margin),
                                           (basis_hbm, basis), (fwd_hbm, fwd_raw), (bwd_hbm, bwd_raw), (col_hbm, col)]):
        loads.append(pltpu.make_async_copy(source, target, load_sem.at[at]))
    for copy in loads[:3]:
        copy.start()

    barrier = pltpu.get_barrier_semaphore()

    def greet(device):
        pl.semaphore_signal(barrier, inc=1, device_id=device, device_id_type=MESH)

    row, chip, core = me_y // 8, lax.rem(me_y // 2, 4), lax.rem(me_y, 2)
    plane = []
    for far in (4, 3, 2, 1, 0):
        for dy in range(4):
            for dx in range(4):
                for dc in range(2):
                    if min(dy, 4 - dy) + min(dx, 4 - dx) == far and (dy, dx, dc) != (0, 0, 0):
                        at = 8 * lax.rem(row + dy, 4) + 2 * lax.rem(chip + dx, 4) + lax.rem(core + dc, 2)
                        plane.append({"fy": at, "fx": me_x})
    line = {}
    for k in range(1, fx_count):
        line[k] = {"fy": me_y, "fx": lax.rem(me_x + k, fx_count)}
    order = sorted(line, key=lambda k: -min(k, fx_count - k))
    is_early, is_late = me_x < EARLY, me_x >= EARLY
    has_left, has_right = me_x > 0, me_x < fx_count - 1

    def greet_many():
        for k in order:
            greet(line[k])
        for device in plane:
            greet(device)

    def greet_few():
        greet({"fy": over, "fx": me_x})
        greet({"fy": below, "fx": me_x})
        greet({"fy": me_y, "fx": left})

    pl.when(is_early)(greet_many)
    pl.when(is_late)(greet_few)
    pl.when(jnp.logical_and(is_late, has_right))(lambda: greet({"fy": me_y, "fx": right}))
    pl.when(has_right)(lambda: greet({"fy": below, "fx": right}))
    pl.when(has_left)(lambda: greet({"fy": over, "fx": left}))

    lane = lax.broadcasted_iota(jnp.int32, (1, COLS), 1)
    block = lane // PAD

    for copy in loads[:3]:
        copy.wait()
    for copy in loads[3:]:
        copy.start()
    energy = jnp.zeros((ROWS, COLS), F32)
    for c in range(CHANNELS):
        value = DUAL_STEP * samp[c] * start[c] - DUAL_STEP * dirty[c]
        shifted_ref[c] = value
        energy = energy + value * value
    energy = jnp.sum(energy, axis=0, keepdims=True)
    line_out[...] = energy

    for g in range(GROUPS):
        total = jnp.zeros((ROWS, COLS), F32)
        for q in range(4):
            value = start[4 * g + q]
            moved = value if q == 3 else pltpu.roll(value, PAD * (q + 1), 1)
            total = jnp.where(block == q, moved, total)
        pack[g] = total
    one = lambda flag: flag.astype(jnp.int32)
    guests = jnp.where(
        is_early,
        len(plane) + EARLY - 1 + one(me_x == EARLY - 1) + one(has_left) + 1,
        2 + EARLY + one(me_x > EARLY) + 1 + 2 * one(has_right))
    pl.semaphore_wait(barrier, guests)

    def line_copy(z):
        return pltpu.make_async_remote_copy(
            src_ref=line_out, dst_ref=line_in.at[me_x], send_sem=line_sem.at[0], recv_sem=line_sem.at[1],
            device_id={"fy": me_y, "fx": z}, device_id_type=MESH)

    for z in range(EARLY):
        pl.when(me_x != z)(lambda z=z: line_copy(z).start())

    halos = []
    for h in range(HALVES):
        chans = pl.ds(h * PER, PER)
        groups = pl.ds(h * PER // 4, PER // 4)
        for at, (source, target, device) in enumerate([
            (start.at[chans], above.at[chans], {"fy": below, "fx": me_x}),
            (pack.at[groups], left_in.at[groups], {"fy": me_y, "fx": right}),
            (pack.at[groups], corner_in.at[groups], {"fy": below, "fx": right}),
        ]):
            copy = pltpu.make_async_remote_copy(
                src_ref=source, dst_ref=target, send_sem=halo_send.at[h, at], recv_sem=halo_recv.at[h, at],
                device_id=device, device_id_type=MESH)
            if at == 0:
                copy.start()
            else:
                pl.when(has_right)(copy.start)
            halos.append(copy)

    def no_left():
        left_in[...] = jnp.zeros_like(left_in)
        corner_in[...] = jnp.zeros_like(corner_in)

    def no_right():
        left_back[...] = jnp.zeros_like(left_back)
        corner_back[...] = jnp.zeros_like(corner_back)

    pl.when(jnp.logical_not(has_left))(no_left)
    pl.when(jnp.logical_not(has_right))(no_right)

    for copy in loads[3:]:
        copy.wait()
    row_has = (me_y > 0).astype(jnp.int32)
    col_has = (me_x > 0).astype(jnp.int32)
    keep_rows = [margin[0, 0, l, 0] * row_has for l in range(LEVELS)]
    keep_cols = [margin[0, 0, l, 1] * col_has for l in range(LEVELS)]

    row_at = lax.broadcasted_iota(jnp.int32, (128, 192), 0)
    col_at = lax.rem(lax.broadcasted_iota(jnp.int32, (128, 192), 1), 64)
    reach = jnp.where(row_at < 64, keep_rows[0], keep_rows[1])
    fwd_m[...] = jnp.where(PAD - col_at <= reach, fwd_raw[...], 0.0).astype(BF)
    row_at = lax.broadcasted_iota(jnp.int32, (64, 384), 0)
    col_at = lax.rem(lax.broadcasted_iota(jnp.int32, (64, 384), 1), 128)
    reach = jnp.where(col_at < 64, keep_rows[0], keep_rows[1])
    bwd_m[...] = jnp.where(PAD - row_at <= reach, bwd_raw[...], 0.0).astype(BF)

    kept = []
    for l in range(LEVELS):
        inside = PAD - lax.rem(lane, PAD) <= keep_cols[l]
        kept.append([jnp.logical_and(inside, block == q) for q in range(4)])

    columns = []
    diagonal = lax.broadcasted_iota(jnp.int32, (CHANNELS, CHANNELS), 0) == lax.broadcasted_iota(jnp.int32, (CHANNELS, CHANNELS), 1)
    for r in range(RANK):
        vector = jnp.sum(jnp.where(diagonal, basis[r : r + 1, :], 0.0), axis=1, keepdims=True)
        vector = jnp.broadcast_to(vector, (CHANNELS, COLS))
        for previous in columns:
            vector = vector - jnp.sum(previous * vector, axis=0, keepdims=True) * previous
        vector = vector / jnp.sqrt(jnp.sum(vector * vector, axis=0, keepdims=True))
        columns.append(vector)
        spec[r] = vector

    def project(field):
        weights = []
        for r in range(RANK):
            total = spec[r, 0:1, :] * field(0)
            for c in range(1, CHANNELS):
                total = total + spec[r, c : c + 1, :] * field(c)
            weights.append(total)

        def channel(c):
            total = spec[0, c : c + 1, :] * weights[0]
            for r in range(1, RANK):
                total = total + spec[r, c : c + 1, :] * weights[r]
            return total

        return channel

    pb = project(lambda c: PRIMAL_STEP * samp[c] * shifted_ref[c])
    for c in range(CHANNELS):
        pb_ref[c] = pb(c)

    def place(target, p, part, row0, value):
        high, low = split(value)
        lanes = pl.ds(COLS * part, COLS)
        target[p, pl.ds(row0, ROWS), lanes] = high
        target[p, pl.ds(64 + row0, ROWS), lanes] = low
        target[p, pl.ds(128 + row0, ROWS), lanes] = high

    for c in range(CHANNELS):
        place(x_own, c // 2, c % 2, PAD, start[c])

    backs = []
    for h in range(HALVES):
        halos[3 * h].wait_recv()

        def from_left(h=h):
            halos[3 * h + 1].wait_recv()
            halos[3 * h + 2].wait_recv()

        pl.when(has_left)(from_left)
        first = h * PER
        for c in range(first, first + PER):
            place(x_own, c // 2, c % 2, 0, above[c])
        for g in range(first // 4, (first + PER) // 4):
            place(x_left, g, 0, 0, corner_in[g])
            place(x_left, g, 0, PAD, left_in[g])
        for p in range(first // 2, (first + PER) // 2):
            u = dot(fwd_m[...], x_own[p])
            high, low = split(u)
            for part in range(2):
                c = 2 * p + part - first
                lanes = slice(COLS * part, COLS * (part + 1))
                for l in range(LEVELS):
                    lhs[l, pl.ds(64 * c, 64), 0:128] = high[64 * l : 64 * l + 64, lanes]
                    lhs[l, pl.ds(64 * c, 64), 256:384] = low[64 * l : 64 * l + 64, lanes]
        for g in range(first // 4, (first + PER) // 4):
            u = dot(fwd_m[...], x_left[g])
            for q in range(4):
                c = 4 * g + q - first
                for l in range(LEVELS):
                    high, low = split(jnp.where(kept[l][q], u[64 * l : 64 * l + 64, :], 0.0))
                    lhs[l, pl.ds(64 * c, 64), 128:256] = high
                    lhs[l, pl.ds(64 * c, 64), 384:512] = low
        z_sum = [[jnp.zeros((64, COLS), F32) for l in range(LEVELS)] for g in range(PER // 4)]
        for l in range(LEVELS):
            acc = dot(lhs[l, :, 0:256], col[l]) + dot(lhs[l, :, 256:512], col[l])
            acc = jnp.clip(acc, -CLIP_LEVEL, CLIP_LEVEL)
            high, low = split(acc)
            for c in range(PER):
                zero = jnp.zeros((32, COLS), BF)
                top, mid, end = 64 * c, 64 * c + 32, 64 * c + 64
                bands[pl.ds(top, 32), 0:128] = zero
                bands[pl.ds(top, 32), 256:384] = zero
                bands[pl.ds(top, 32), 128:256] = high[top:mid, 128:256]
                bands[pl.ds(top, 32), 384:512] = low[top:mid, 128:256]
                bands[pl.ds(mid, 32), 0:256] = high[mid:end, :]
                bands[pl.ds(mid, 32), 256:512] = low[mid:end, :]
            z = dot(bands[:, 0:256], col[LEVELS + l]) + dot(bands[:, 256:512], col[LEVELS + l])
            for c in range(PER):
                high, low = split(z[64 * c : 64 * c + 64, 0:128])
                lanes = pl.ds(COLS * (c % 2), COLS)
                z_own[c // 2, pl.ds(64 * l, 64), lanes] = high
                z_own[c // 2, pl.ds(128 + 64 * l, 64), lanes] = low
                piece = z[64 * c : 64 * c + 64, 128:256]
                z_sum[c // 4][l] = z_sum[c // 4][l] + jnp.where(kept[l][c % 4], piece, 0.0)
        for g in range(PER // 4):
            for l in range(LEVELS):
                high, low = split(z_sum[g][l])
                z_left[g, pl.ds(64 * l, 64), :] = high
                z_left[g, pl.ds(128 + 64 * l, 64), :] = low
            left_out[first // 4 + g] = dot(bwd_m[:, 0:256], z_left[g]) + dot(bwd_m[:, 256:384], z_left[g, 0:128, :])
        for p in range(PER // 2):
            r = dot(bwd_m[:, 0:256], z_own[p]) + dot(bwd_m[:, 256:384], z_own[p, 0:128, :])
            for part in range(2):
                c = first + 2 * p + part
                up_out[c] = r[0:32, COLS * part : COLS * (part + 1)]
                own[c] = r[32:64, COLS * part : COLS * (part + 1)]
        chans = pl.ds(first, PER)
        groups = pl.ds(first // 4, PER // 4)
        for at, (source, target, device) in enumerate([
            (left_out.at[groups, pl.ds(32, 32), :], left_back.at[groups], {"fy": me_y, "fx": left}),
            (left_out.at[groups, pl.ds(0, 32), :], corner_back.at[groups], {"fy": over, "fx": left}),
            (up_out.at[chans], up_in.at[chans], {"fy": over, "fx": me_x}),
        ]):
            copy = pltpu.make_async_remote_copy(
                src_ref=source, dst_ref=target, send_sem=back_send.at[h, at], recv_sem=back_recv.at[h, at],
                device_id=device, device_id_type=MESH)
            if at == 2:
                copy.start()
            else:
                pl.when(has_left)(copy.start)
            backs.append(copy)

    def exchange():
        pltpu.make_async_copy(line_in.at[pl.ds(0, fx_count - 1)], line_in.at[pl.ds(0, fx_count - 1)], line_sem.at[1]).wait()
        line_in[me_x] = line_out[...]
        partial = jnp.sum(line_in[...], axis=0)
        plane_out[...] = partial
        plane_in[me_y] = partial
        for device in plane:
            pltpu.make_async_remote_copy(
                src_ref=plane_out, dst_ref=plane_in.at[me_y], send_sem=plane_sem.at[0], recv_sem=plane_sem.at[1],
                device_id=device, device_id_type=MESH).start()

    pl.when(is_early)(exchange)

    for at, copy in enumerate(backs):
        if at % 3 == 2:
            copy.wait_recv()
        else:
            pl.when(has_right)(copy.wait_recv)
    for g in range(GROUPS):
        strip = left_back[g] + corner_back[g]
        for q in range(4):
            c = 4 * g + q
            moved = strip if q == 3 else pltpu.roll(strip, COLS - PAD * (q + 1), 1)
            own[c] = start[c] - (own[c] + up_in[c] + jnp.where(block == 3, moved, 0.0))
    pa = project(lambda c: own[c])
    for c in range(CHANNELS):
        pa_ref[c] = pa(c)

    def total_copy(z):
        return pltpu.make_async_remote_copy(
            src_ref=total_out, dst_ref=total_in, send_sem=total_sem.at[0], recv_sem=total_sem.at[1],
            device_id={"fy": me_y, "fx": z}, device_id_type=MESH)

    middle = (EARLY - 1 + fx_count) // 2 + 1
    shares = {0: range(fx_count - 1, middle - 1, -1), EARLY - 1: range(EARLY, middle)}

    def finish():
        pltpu.make_async_copy(plane_in.at[pl.ds(0, fy_count - 1)], plane_in.at[pl.ds(0, fy_count - 1)], plane_sem.at[1]).wait()
        total = jnp.sum(plane_in[...], axis=0)
        total_in[...] = total
        total_out[...] = total

    def hand(zs):
        for z in zs:
            total_copy(z).start()

    pl.when(is_early)(finish)
    for z, zs in shares.items():
        pl.when(me_x == z)(functools.partial(hand, zs))
    pl.when(is_late)(lambda: total_copy(0).wait_recv())
    total = jnp.sum(total_in[...], axis=1, keepdims=True)
    radius = BALL_SCALE * math.sqrt(CHANNELS * ROWS * COLS * fy_count * fx_count)
    factor = jnp.maximum(0.0, 1.0 - DUAL_STEP * radius / jnp.sqrt(total + NORM_EPS))
    factor_ref[...] = jnp.broadcast_to(factor, (1, COLS))

    for at, copy in enumerate(halos):
        if at % 3 == 0:
            copy.wait_send()
        else:
            pl.when(has_right)(copy.wait_send)
    for at, copy in enumerate(backs):
        if at % 3 == 2:
            copy.wait_send()
        else:
            pl.when(has_left)(copy.wait_send)

    def sent(ref, count, sem):
        pltpu.make_async_copy(ref.at[pl.ds(0, count)], ref.at[pl.ds(0, count)], sem).wait()

    def early_sent():
        sent(line_in, EARLY - 1, line_sem.at[0])
        sent(plane_in, fy_count - 1, plane_sem.at[0])

    pl.when(is_early)(early_sent)
    pl.when(is_late)(lambda: sent(line_in, EARLY, line_sem.at[0]))
    for z, zs in shares.items():
        pl.when(me_x == z)(functools.partial(sent, line_in, len(zs), total_sem.at[0]))


def per_device(fy_count, fx_count, start_image, dirty, sampling, basis_seed, margin):
    forward, backward, column = tables()
    tile = jax.ShapeDtypeStruct((CHANNELS, ROWS, COLS), F32)
    hbm = pl.BlockSpec(memory_space=pltpu.HBM)
    vmem = pl.BlockSpec(memory_space=pltpu.VMEM)
    field = pltpu.VMEM((CHANNELS, ROWS, COLS), F32)
    strips = pltpu.VMEM((GROUPS, ROWS, COLS), F32)
    dma = pltpu.SemaphoreType.DMA

    def body(*refs):
        kernel_body(fy_count, fx_count, *refs)

    pa, pb, shifted, factor = pl.pallas_call(
        body,
        out_shape=(tile, tile, tile, jax.ShapeDtypeStruct((1, COLS), F32)),
        in_specs=[hbm] * 8,
        out_specs=(vmem,) * 4,
        scratch_shapes=[
            field, field, field,
            pltpu.VMEM((RANK, CHANNELS), F32),
            pltpu.SMEM((1, 1, LEVELS, 2), jnp.int32),
            pltpu.VMEM((128, 192), F32), pltpu.VMEM((64, 384), F32), pltpu.VMEM((2 * LEVELS, 256, 256), BF),
            pltpu.VMEM((128, 192), BF), pltpu.VMEM((64, 384), BF),
            strips, field, strips, strips,
            pltpu.VMEM((CHANNELS // 2, 192, 256), BF), pltpu.VMEM((GROUPS, 192, COLS), BF),
            pltpu.VMEM((LEVELS, 64 * PER, 512), BF), pltpu.VMEM((64 * PER, 512), BF),
            pltpu.VMEM((PER // 2, 256, 256), BF), pltpu.VMEM((PER // 4, 256, COLS), BF),
            field, field, pltpu.VMEM((GROUPS, 64, COLS), F32), field, strips, strips,
            pltpu.VMEM((RANK, CHANNELS, COLS), F32),
            pltpu.VMEM((1, COLS), F32), pltpu.VMEM((fx_count, 1, COLS), F32),
            pltpu.VMEM((1, COLS), F32), pltpu.VMEM((fy_count, 1, COLS), F32),
            pltpu.VMEM((1, COLS), F32), pltpu.VMEM((1, COLS), F32),
            dma((8,)), dma((HALVES, 3)), dma((HALVES, 3)), dma((2,)), dma((2,)), dma((2,)), dma((HALVES, 3)), dma((HALVES, 3)),
        ],
        compiler_params=pltpu.CompilerParams(collective_id=0, has_side_effects=True, vmem_limit_bytes=40 * 1024 * 1024),
        name="step",
    )(*(pltpu.with_memory_space_constraint(value, pltpu.HBM) for value in (
        start_image, dirty, sampling, basis_seed.T, margin,
        jnp.asarray(forward, F32), jnp.asarray(backward, F32), jnp.asarray(column, BF))))
    factor = factor[0, 0]
    return jnp.maximum(pa - factor * pb, 0.0), factor * shifted


def solution(mesh):
    fy_count, fx_count = mesh.shape["fy"], mesh.shape["fx"]

    def step(*args):
        return per_device(fy_count, fx_count, *args)

    image = P(None, "fy", "fx")
    return jax.shard_map(
        step, mesh=mesh, in_specs=(image, image, image, P(), P("fy", "fx", None, None)),
        out_specs=(image, image), check_vma=False)
```

```python
import functools
import math

import jax
import jax.numpy as jnp
import numpy as np
from jax import lax
from jax.experimental import pallas as pl
from jax.experimental.pallas import tpu as pltpu
from jax.sharding import PartitionSpec as P

MESH = pl.DeviceIdType.MESH
BF = jnp.bfloat16
F32 = jnp.float32

LEVELS = 2
PAD = 32
ROWS = 32
COLS = 128
CHANNELS = 16
RANK = 4
HALVES = 2
EARLY = 4
PER = CHANNELS // HALVES
GROUPS = CHANNELS // 4


DAUBECHIES = [
    -0.00011747678400228192,
    0.0006754494059985568,
    -0.0003917403729959771,
    -0.00487035299301066,
    0.008746094047015655,
    0.013981027917015516,
    -0.04408825393106472,
    -0.01736930100202211,
    0.128747426620186,
    0.00047248457399797254,
    -0.2840155429624281,
    -0.015829105256023893,
    0.5853546836548691,
    0.6756307362980128,
    0.3128715909144659,
    0.05441584224308161,
]
DUAL_STEP = 0.5
PRIMAL_STEP = 0.5
CLIP_LEVEL = 0.08
BALL_SCALE = 0.8
NORM_EPS = 1e-06


def taps_pair():
    low = [tap / math.sqrt(2.0) for tap in DAUBECHIES]
    high = [(-1.0) ** k * low[len(low) - 1 - k] for k in range(len(low))]
    return low, high


def band_matrix(taps, extent, dilation):
    matrix = np.zeros((extent + PAD, extent), np.float64)
    for k, tap in enumerate(taps):
        for i in range(extent):
            matrix[i + PAD - k * dilation, i] += tap
    return matrix


def split_host(matrix):
    high = matrix.astype(np.float32).astype(jnp.bfloat16)
    low = (matrix - high.astype(np.float64)).astype(np.float32).astype(jnp.bfloat16)
    return high, low


def tables():
    low, high = taps_pair()
    scale = DUAL_STEP / math.sqrt(LEVELS)
    rows, cols = [], []
    for level in range(LEVELS):
        d = 2**level
        rows.append(band_matrix(low, ROWS, d).T)
        rows.append(band_matrix(high, ROWS, d).T)
        both = np.concatenate([band_matrix(low, COLS, d), band_matrix(high, COLS, d)], axis=1) * scale
        cols.append(np.concatenate([both[PAD:]] + [both[:PAD]] * 4, axis=0))
    row_all = np.concatenate(rows, axis=0)
    hi, lo = (part.astype(np.float32) for part in split_host(row_all))
    forward = np.concatenate([hi, hi, lo], axis=1)
    backward = np.concatenate([hi.T, hi.T, lo.T], axis=1)
    column = []
    for level in range(LEVELS):
        column.append(split_host(cols[level])[0])
    for level in range(LEVELS):
        column.append(split_host(cols[level].T)[0])
    return forward, backward, np.stack(column)


def split(value):
    high = value.astype(BF)
    return high, (value - high.astype(F32)).astype(BF)


def dot(a, b):
    return jnp.dot(a, b, preferred_element_type=F32)


def kernel_body(fy_count, fx_count, start_hbm, dirty_hbm, samp_hbm, basis_hbm, margin_hbm, fwd_hbm, bwd_hbm, col_hbm,
                pa_ref, pb_ref, shifted_ref, factor_ref,
                start, dirty, samp, basis, margin, fwd_raw, bwd_raw, col,
                fwd_m, bwd_m, pack, above, left_in, corner_in,
                x_own, x_left, lhs, bands, z_own, z_left, own, up_out, left_out, up_in, left_back, corner_back,
                spec, line_out, line_in, plane_out, plane_in, total_out, total_in,
                input_sem, load_sem, halo_send, halo_recv, line_sem, plane_sem, total_sem, back_send, back_recv):
    me_y, me_x = lax.axis_index("fy"), lax.axis_index("fx")
    below, over = lax.rem(me_y + 1, fy_count), lax.rem(me_y + fy_count - 1, fy_count)
    right, left = lax.rem(me_x + 1, fx_count), lax.rem(me_x + fx_count - 1, fx_count)

    loads = []
    for at, (source, target) in enumerate([(margin_hbm, margin), (basis_hbm, basis), (fwd_hbm, fwd_raw), (bwd_hbm, bwd_raw), (col_hbm, col)]):
        loads.append(pltpu.make_async_copy(source, target, load_sem.at[at]))
    quarters = []
    for part in range(4):
        chans = pl.ds(4 * part, 4)
        quarters.append([])
        for at, (source, target) in enumerate([(start_hbm, start), (dirty_hbm, dirty), (samp_hbm, samp)]):
            copy = pltpu.make_async_copy(source.at[chans], target.at[chans], input_sem.at[part, at])
            copy.start()
            quarters[part].append(copy)

    barrier = pltpu.get_barrier_semaphore()

    def greet(device):
        pl.semaphore_signal(barrier, inc=1, device_id=device, device_id_type=MESH)

    row, chip, core = me_y // 8, lax.rem(me_y // 2, 4), lax.rem(me_y, 2)
    plane = []
    for far in (4, 3, 2, 1, 0):
        for dy in range(4):
            for dx in range(4):
                for dc in range(2):
                    if min(dy, 4 - dy) + min(dx, 4 - dx) == far and (dy, dx, dc) != (0, 0, 0):
                        at = 8 * lax.rem(row + dy, 4) + 2 * lax.rem(chip + dx, 4) + lax.rem(core + dc, 2)
                        plane.append({"fy": at, "fx": me_x})
    line = {}
    for k in range(1, fx_count):
        line[k] = {"fy": me_y, "fx": lax.rem(me_x + k, fx_count)}
    order = sorted(line, key=lambda k: -min(k, fx_count - k))
    is_early, is_late = me_x < EARLY, me_x >= EARLY
    has_left, has_right = me_x > 0, me_x < fx_count - 1

    def greet_many():
        for k in order:
            greet(line[k])
        for device in plane:
            greet(device)

    def greet_few():
        greet({"fy": over, "fx": me_x})
        greet({"fy": below, "fx": me_x})
        greet({"fy": me_y, "fx": left})

    pl.when(is_early)(greet_many)
    pl.when(is_late)(greet_few)
    pl.when(jnp.logical_and(is_late, has_right))(lambda: greet({"fy": me_y, "fx": right}))
    pl.when(has_right)(lambda: greet({"fy": below, "fx": right}))
    pl.when(has_left)(lambda: greet({"fy": over, "fx": left}))

    lane = lax.broadcasted_iota(jnp.int32, (1, COLS), 1)
    block = lane // PAD

    energy = jnp.zeros((ROWS, COLS), F32)
    for c in range(CHANNELS):
        if c % 4 == 0:
            for copy in quarters[c // 4]:
                copy.wait()
        value = DUAL_STEP * samp[c] * start[c] - DUAL_STEP * dirty[c]
        shifted_ref[c] = value
        energy = energy + value * value
    energy = jnp.sum(energy, axis=0, keepdims=True)
    line_out[...] = energy

    one = lambda flag: flag.astype(jnp.int32)
    guests = jnp.where(
        is_early,
        len(plane) + EARLY - 1 + one(me_x == EARLY - 1) + one(has_left) + 1,
        2 + EARLY + one(me_x > EARLY) + 1 + 2 * one(has_right))
    pl.semaphore_wait(barrier, guests)

    def line_copy(z):
        return pltpu.make_async_remote_copy(
            src_ref=line_out, dst_ref=line_in.at[me_x], send_sem=line_sem.at[0], recv_sem=line_sem.at[1],
            device_id={"fy": me_y, "fx": z}, device_id_type=MESH)

    for z in range(EARLY):
        pl.when(me_x != z)(lambda z=z: line_copy(z).start())

    for copy in loads:
        copy.start()
    for g in range(GROUPS):
        total = jnp.zeros((ROWS, COLS), F32)
        for q in range(4):
            value = start[4 * g + q]
            moved = value if q == 3 else pltpu.roll(value, PAD * (q + 1), 1)
            total = jnp.where(block == q, moved, total)
        pack[g] = total

    halos = []
    for h in range(HALVES):
        chans = pl.ds(h * PER, PER)
        groups = pl.ds(h * PER // 4, PER // 4)
        for at, (source, target, device) in enumerate([
            (start.at[chans], above.at[chans], {"fy": below, "fx": me_x}),
            (pack.at[groups], left_in.at[groups], {"fy": me_y, "fx": right}),
            (pack.at[groups], corner_in.at[groups], {"fy": below, "fx": right}),
        ]):
            copy = pltpu.make_async_remote_copy(
                src_ref=source, dst_ref=target, send_sem=halo_send.at[h, at], recv_sem=halo_recv.at[h, at],
                device_id=device, device_id_type=MESH)
            if at == 0:
                copy.start()
            else:
                pl.when(has_right)(copy.start)
            halos.append(copy)

    def no_left():
        left_in[...] = jnp.zeros_like(left_in)
        corner_in[...] = jnp.zeros_like(corner_in)

    def no_right():
        left_back[...] = jnp.zeros_like(left_back)
        corner_back[...] = jnp.zeros_like(corner_back)

    pl.when(jnp.logical_not(has_left))(no_left)
    pl.when(jnp.logical_not(has_right))(no_right)

    for copy in loads:
        copy.wait()
    row_has = (me_y > 0).astype(jnp.int32)
    col_has = (me_x > 0).astype(jnp.int32)
    keep_rows = [margin[0, 0, l, 0] * row_has for l in range(LEVELS)]
    keep_cols = [margin[0, 0, l, 1] * col_has for l in range(LEVELS)]

    row_at = lax.broadcasted_iota(jnp.int32, (128, 192), 0)
    col_at = lax.rem(lax.broadcasted_iota(jnp.int32, (128, 192), 1), 64)
    reach = jnp.where(row_at < 64, keep_rows[0], keep_rows[1])
    fwd_m[...] = jnp.where(PAD - col_at <= reach, fwd_raw[...], 0.0).astype(BF)
    row_at = lax.broadcasted_iota(jnp.int32, (64, 384), 0)
    col_at = lax.rem(lax.broadcasted_iota(jnp.int32, (64, 384), 1), 128)
    reach = jnp.where(col_at < 64, keep_rows[0], keep_rows[1])
    bwd_m[...] = jnp.where(PAD - row_at <= reach, bwd_raw[...], 0.0).astype(BF)

    kept = []
    for l in range(LEVELS):
        inside = PAD - lax.rem(lane, PAD) <= keep_cols[l]
        kept.append([jnp.logical_and(inside, block == q) for q in range(4)])

    columns = []
    diagonal = lax.broadcasted_iota(jnp.int32, (CHANNELS, CHANNELS), 0) == lax.broadcasted_iota(jnp.int32, (CHANNELS, CHANNELS), 1)
    for r in range(RANK):
        vector = jnp.sum(jnp.where(diagonal, basis[r : r + 1, :], 0.0), axis=1, keepdims=True)
        vector = jnp.broadcast_to(vector, (CHANNELS, COLS))
        for previous in columns:
            vector = vector - jnp.sum(previous * vector, axis=0, keepdims=True) * previous
        vector = vector / jnp.sqrt(jnp.sum(vector * vector, axis=0, keepdims=True))
        columns.append(vector)
        spec[r] = vector

    def project(field):
        weights = []
        for r in range(RANK):
            total = spec[r, 0:1, :] * field(0)
            for c in range(1, CHANNELS):
                total = total + spec[r, c : c + 1, :] * field(c)
            weights.append(total)

        def channel(c):
            total = spec[0, c : c + 1, :] * weights[0]
            for r in range(1, RANK):
                total = total + spec[r, c : c + 1, :] * weights[r]
            return total

        return channel

    pb = project(lambda c: PRIMAL_STEP * samp[c] * shifted_ref[c])
    for c in range(CHANNELS):
        pb_ref[c] = pb(c)

    def place(target, p, part, row0, value):
        high, low = split(value)
        lanes = pl.ds(COLS * part, COLS)
        target[p, pl.ds(row0, ROWS), lanes] = high
        target[p, pl.ds(64 + row0, ROWS), lanes] = low
        target[p, pl.ds(128 + row0, ROWS), lanes] = high

    for c in range(CHANNELS):
        place(x_own, c // 2, c % 2, PAD, start[c])

    backs = []
    for h in range(HALVES):
        halos[3 * h].wait_recv()

        def from_left(h=h):
            halos[3 * h + 1].wait_recv()
            halos[3 * h + 2].wait_recv()

        pl.when(has_left)(from_left)
        first = h * PER
        for c in range(first, first + PER):
            place(x_own, c // 2, c % 2, 0, above[c])
        for g in range(first // 4, (first + PER) // 4):
            place(x_left, g, 0, 0, corner_in[g])
            place(x_left, g, 0, PAD, left_in[g])
        for p in range(first // 2, (first + PER) // 2):
            u = dot(fwd_m[...], x_own[p])
            high, low = split(u)
            for part in range(2):
                c = 2 * p + part - first
                lanes = slice(COLS * part, COLS * (part + 1))
                for l in range(LEVELS):
                    lhs[l, pl.ds(64 * c, 64), 0:128] = high[64 * l : 64 * l + 64, lanes]
                    lhs[l, pl.ds(64 * c, 64), 256:384] = low[64 * l : 64 * l + 64, lanes]
        for g in range(first // 4, (first + PER) // 4):
            u = dot(fwd_m[...], x_left[g])
            for q in range(4):
                c = 4 * g + q - first
                for l in range(LEVELS):
                    high, low = split(jnp.where(kept[l][q], u[64 * l : 64 * l + 64, :], 0.0))
                    lhs[l, pl.ds(64 * c, 64), 128:256] = high
                    lhs[l, pl.ds(64 * c, 64), 384:512] = low
        z_sum = [[jnp.zeros((64, COLS), F32) for l in range(LEVELS)] for g in range(PER // 4)]
        for l in range(LEVELS):
            acc = dot(lhs[l, :, 0:256], col[l]) + dot(lhs[l, :, 256:512], col[l])
            acc = jnp.clip(acc, -CLIP_LEVEL, CLIP_LEVEL)
            high, low = split(acc)
            for c in range(PER):
                zero = jnp.zeros((32, COLS), BF)
                top, mid, end = 64 * c, 64 * c + 32, 64 * c + 64
                bands[pl.ds(top, 32), 0:128] = zero
                bands[pl.ds(top, 32), 256:384] = zero
                bands[pl.ds(top, 32), 128:256] = high[top:mid, 128:256]
                bands[pl.ds(top, 32), 384:512] = low[top:mid, 128:256]
                bands[pl.ds(mid, 32), 0:256] = high[mid:end, :]
                bands[pl.ds(mid, 32), 256:512] = low[mid:end, :]
            z = dot(bands[:, 0:256], col[LEVELS + l]) + dot(bands[:, 256:512], col[LEVELS + l])
            for c in range(PER):
                high, low = split(z[64 * c : 64 * c + 64, 0:128])
                lanes = pl.ds(COLS * (c % 2), COLS)
                z_own[c // 2, pl.ds(64 * l, 64), lanes] = high
                z_own[c // 2, pl.ds(128 + 64 * l, 64), lanes] = low
                piece = z[64 * c : 64 * c + 64, 128:256]
                z_sum[c // 4][l] = z_sum[c // 4][l] + jnp.where(kept[l][c % 4], piece, 0.0)
        for g in range(PER // 4):
            for l in range(LEVELS):
                high, low = split(z_sum[g][l])
                z_left[g, pl.ds(64 * l, 64), :] = high
                z_left[g, pl.ds(128 + 64 * l, 64), :] = low
            left_out[first // 4 + g] = dot(bwd_m[:, 0:256], z_left[g]) + dot(bwd_m[:, 256:384], z_left[g, 0:128, :])
        for p in range(PER // 2):
            r = dot(bwd_m[:, 0:256], z_own[p]) + dot(bwd_m[:, 256:384], z_own[p, 0:128, :])
            for part in range(2):
                c = first + 2 * p + part
                up_out[c] = r[0:32, COLS * part : COLS * (part + 1)]
                own[c] = r[32:64, COLS * part : COLS * (part + 1)]
        chans = pl.ds(first, PER)
        groups = pl.ds(first // 4, PER // 4)
        for at, (source, target, device) in enumerate([
            (left_out.at[groups, pl.ds(32, 32), :], left_back.at[groups], {"fy": me_y, "fx": left}),
            (left_out.at[groups, pl.ds(0, 32), :], corner_back.at[groups], {"fy": over, "fx": left}),
            (up_out.at[chans], up_in.at[chans], {"fy": over, "fx": me_x}),
        ]):
            copy = pltpu.make_async_remote_copy(
                src_ref=source, dst_ref=target, send_sem=back_send.at[h, at], recv_sem=back_recv.at[h, at],
                device_id=device, device_id_type=MESH)
            if at == 2:
                copy.start()
            else:
                pl.when(has_left)(copy.start)
            backs.append(copy)

    def exchange():
        pltpu.make_async_copy(line_in.at[pl.ds(0, fx_count - 1)], line_in.at[pl.ds(0, fx_count - 1)], line_sem.at[1]).wait()
        line_in[me_x] = line_out[...]
        partial = jnp.sum(line_in[...], axis=0)
        plane_out[...] = partial
        plane_in[me_y] = partial
        for device in plane:
            pltpu.make_async_remote_copy(
                src_ref=plane_out, dst_ref=plane_in.at[me_y], send_sem=plane_sem.at[0], recv_sem=plane_sem.at[1],
                device_id=device, device_id_type=MESH).start()

    pl.when(is_early)(exchange)

    for at, copy in enumerate(backs):
        if at % 3 == 2:
            copy.wait_recv()
        else:
            pl.when(has_right)(copy.wait_recv)
    for g in range(GROUPS):
        strip = left_back[g] + corner_back[g]
        for q in range(4):
            c = 4 * g + q
            moved = strip if q == 3 else pltpu.roll(strip, COLS - PAD * (q + 1), 1)
            own[c] = start[c] - (own[c] + up_in[c] + jnp.where(block == 3, moved, 0.0))
    pa = project(lambda c: own[c])
    for c in range(CHANNELS):
        pa_ref[c] = pa(c)

    def total_copy(z):
        return pltpu.make_async_remote_copy(
            src_ref=total_out, dst_ref=total_in, send_sem=total_sem.at[0], recv_sem=total_sem.at[1],
            device_id={"fy": me_y, "fx": z}, device_id_type=MESH)

    middle = (EARLY - 1 + fx_count) // 2 + 1
    shares = {EARLY - 2: range(fx_count - 1, middle, -1), EARLY - 1: range(EARLY, middle + 1)}

    def finish():
        pltpu.make_async_copy(plane_in.at[pl.ds(0, fy_count - 1)], plane_in.at[pl.ds(0, fy_count - 1)], plane_sem.at[1]).wait()
        total = jnp.sum(plane_in[...], axis=0)
        total_in[...] = total
        total_out[...] = total

    def hand(zs):
        for z in zs:
            total_copy(z).start()

    for at, copy in enumerate(halos):
        if at % 3 == 0:
            copy.wait_send()
        else:
            pl.when(has_right)(copy.wait_send)
    for at, copy in enumerate(backs):
        if at % 3 == 2:
            copy.wait_send()
        else:
            pl.when(has_left)(copy.wait_send)

    def sent(ref, count, sem):
        pltpu.make_async_copy(ref.at[pl.ds(0, count)], ref.at[pl.ds(0, count)], sem).wait()

    def early_sent():
        sent(line_in, EARLY - 1, line_sem.at[0])
        sent(plane_in, fy_count - 1, plane_sem.at[0])

    pl.when(is_early)(early_sent)
    pl.when(is_late)(lambda: sent(line_in, EARLY, line_sem.at[0]))

    pl.when(is_early)(finish)
    pl.when(is_late)(lambda: total_copy(0).wait_recv())
    total = jnp.sum(total_in[...], axis=1, keepdims=True)
    radius = BALL_SCALE * math.sqrt(CHANNELS * ROWS * COLS * fy_count * fx_count)
    factor = jnp.maximum(0.0, 1.0 - DUAL_STEP * radius / jnp.sqrt(total + NORM_EPS))
    factor_ref[...] = jnp.broadcast_to(factor, (1, COLS))

    for z, zs in shares.items():
        pl.when(me_x == z)(functools.partial(hand, zs))
    for z, zs in shares.items():
        pl.when(me_x == z)(functools.partial(sent, line_in, len(zs), total_sem.at[0]))


def last_step(pa_ref, pb_ref, shifted_ref, factor_ref, image_hbm, dual_hbm, image, dual, sems):
    factor = factor_ref[...]
    copies = []
    for part in range(4):
        for c in range(4 * part, 4 * part + 4):
            image[c] = jnp.maximum(pa_ref[c] - factor * pb_ref[c], 0.0)
            dual[c] = factor * shifted_ref[c]
        chans = pl.ds(4 * part, 4)
        for at, (source, target) in enumerate([(image, image_hbm), (dual, dual_hbm)]):
            copy = pltpu.make_async_copy(source.at[chans], target.at[chans], sems.at[part, at])
            copy.start()
            copies.append(copy)
    for copy in copies:
        copy.wait()


def per_device(fy_count, fx_count, start_image, dirty, sampling, basis_seed, margin):
    forward, backward, column = tables()
    tile = jax.ShapeDtypeStruct((CHANNELS, ROWS, COLS), F32)
    hbm = pl.BlockSpec(memory_space=pltpu.HBM)
    vmem = pl.BlockSpec(memory_space=pltpu.VMEM)
    field = pltpu.VMEM((CHANNELS, ROWS, COLS), F32)
    strips = pltpu.VMEM((GROUPS, ROWS, COLS), F32)
    dma = pltpu.SemaphoreType.DMA

    def body(*refs):
        kernel_body(fy_count, fx_count, *refs)

    pa, pb, shifted, factor = pl.pallas_call(
        body,
        out_shape=(tile, tile, tile, jax.ShapeDtypeStruct((1, COLS), F32)),
        in_specs=[hbm] * 8,
        out_specs=(vmem,) * 4,
        scratch_shapes=[
            field, field, field,
            pltpu.VMEM((RANK, CHANNELS), F32),
            pltpu.SMEM((1, 1, LEVELS, 2), jnp.int32),
            pltpu.VMEM((128, 192), F32), pltpu.VMEM((64, 384), F32), pltpu.VMEM((2 * LEVELS, 256, 256), BF),
            pltpu.VMEM((128, 192), BF), pltpu.VMEM((64, 384), BF),
            strips, field, strips, strips,
            pltpu.VMEM((CHANNELS // 2, 192, 256), BF), pltpu.VMEM((GROUPS, 192, COLS), BF),
            pltpu.VMEM((LEVELS, 64 * PER, 512), BF), pltpu.VMEM((64 * PER, 512), BF),
            pltpu.VMEM((PER // 2, 256, 256), BF), pltpu.VMEM((PER // 4, 256, COLS), BF),
            field, field, pltpu.VMEM((GROUPS, 64, COLS), F32), field, strips, strips,
            pltpu.VMEM((RANK, CHANNELS, COLS), F32),
            pltpu.VMEM((1, COLS), F32), pltpu.VMEM((fx_count, 1, COLS), F32),
            pltpu.VMEM((1, COLS), F32), pltpu.VMEM((fy_count, 1, COLS), F32),
            pltpu.VMEM((1, COLS), F32), pltpu.VMEM((1, COLS), F32),
            dma((4, 3)), dma((5,)), dma((HALVES, 3)), dma((HALVES, 3)), dma((2,)), dma((2,)), dma((2,)), dma((HALVES, 3)), dma((HALVES, 3)),
        ],
        compiler_params=pltpu.CompilerParams(collective_id=0, has_side_effects=True, vmem_limit_bytes=40 * 1024 * 1024),
        name="step",
    )(*(pltpu.with_memory_space_constraint(value, pltpu.HBM) for value in (
        start_image, dirty, sampling, basis_seed.T, margin,
        jnp.asarray(forward, F32), jnp.asarray(backward, F32), jnp.asarray(column, BF))))
    return pl.pallas_call(
        last_step,
        out_shape=(tile, tile),
        in_specs=[vmem] * 4,
        out_specs=(hbm, hbm),
        scratch_shapes=[field, field, dma((4, 2))],
        compiler_params=pltpu.CompilerParams(vmem_limit_bytes=4 * 1024 * 1024),
        name="last",
    )(pa, pb, shifted, factor)


def solution(mesh):
    fy_count, fx_count = mesh.shape["fy"], mesh.shape["fx"]

    def step(*args):
        return per_device(fy_count, fx_count, *args)

    image = P(None, "fy", "fx")
    return jax.shard_map(
        step, mesh=mesh, in_specs=(image, image, image, P(), P("fy", "fx", None, None)),
        out_specs=(image, image), check_vma=False)
```

```python
import functools
import math

import jax
import jax.numpy as jnp
import numpy as np
from jax import lax
from jax.experimental import pallas as pl
from jax.experimental.pallas import tpu as pltpu
from jax.sharding import PartitionSpec as P

MESH = pl.DeviceIdType.MESH
BF = jnp.bfloat16
F32 = jnp.float32

LEVELS = 2
PAD = 32
ROWS = 32
COLS = 128
CHANNELS = 16
RANK = 4
HALVES = 2
EARLY = 4
FIRST = 1
FAR = 4
PER = CHANNELS // HALVES
GROUPS = CHANNELS // 4


DAUBECHIES = [
    -0.00011747678400228192,
    0.0006754494059985568,
    -0.0003917403729959771,
    -0.00487035299301066,
    0.008746094047015655,
    0.013981027917015516,
    -0.04408825393106472,
    -0.01736930100202211,
    0.128747426620186,
    0.00047248457399797254,
    -0.2840155429624281,
    -0.015829105256023893,
    0.5853546836548691,
    0.6756307362980128,
    0.3128715909144659,
    0.05441584224308161,
]
DUAL_STEP = 0.5
PRIMAL_STEP = 0.5
CLIP_LEVEL = 0.08
BALL_SCALE = 0.8
NORM_EPS = 1e-06


def taps_pair():
    low = [tap / math.sqrt(2.0) for tap in DAUBECHIES]
    high = [(-1.0) ** k * low[len(low) - 1 - k] for k in range(len(low))]
    return low, high


def band_matrix(taps, extent, dilation):
    matrix = np.zeros((extent + PAD, extent), np.float64)
    for k, tap in enumerate(taps):
        for i in range(extent):
            matrix[i + PAD - k * dilation, i] += tap
    return matrix


def split_host(matrix):
    high = matrix.astype(np.float32).astype(jnp.bfloat16)
    low = (matrix - high.astype(np.float64)).astype(np.float32).astype(jnp.bfloat16)
    return high, low


def tables():
    low, high = taps_pair()
    scale = DUAL_STEP / math.sqrt(LEVELS)
    rows, cols = [], []
    for level in range(LEVELS):
        d = 2**level
        rows.append(band_matrix(low, ROWS, d).T)
        rows.append(band_matrix(high, ROWS, d).T)
        both = np.concatenate([band_matrix(low, COLS, d), band_matrix(high, COLS, d)], axis=1) * scale
        cols.append(np.concatenate([both[PAD:]] + [both[:PAD]] * 4, axis=0))
    row_all = np.concatenate(rows, axis=0)
    hi, lo = (part.astype(np.float32) for part in split_host(row_all))
    forward = np.concatenate([hi, hi, lo], axis=1)
    backward = np.concatenate([hi.T, hi.T, lo.T], axis=1)
    column = []
    for level in range(LEVELS):
        column.append(split_host(cols[level])[0])
    for level in range(LEVELS):
        column.append(split_host(cols[level].T)[0])
    return forward, backward, np.stack(column)


def split(value):
    high = value.astype(BF)
    return high, (value - high.astype(F32)).astype(BF)


def dot(a, b):
    return jnp.dot(a, b, preferred_element_type=F32)


def kernel_body(fy_count, fx_count, start_hbm, dirty_hbm, samp_hbm, basis_hbm, margin_hbm, fwd_hbm, bwd_hbm, col_hbm,
                pa_ref, pb_ref, shifted_ref, factor_ref,
                start, dirty, samp, basis, margin, fwd_raw, bwd_raw, col,
                fwd_m, bwd_m, pack, above, left_in, corner_in,
                x_own, x_left, lhs, bands, z_own, z_left, own, up_out, left_out, up_in, left_back, corner_back,
                spec, line_out, line_in, plane_out, plane_in, side_out, direct_in, total_out, total_in,
                input_sem, load_sem, halo_send, halo_recv, line_sem, plane_sem, direct_sem, total_sem, back_send, back_recv):
    me_y, me_x = lax.axis_index("fy"), lax.axis_index("fx")
    below, over = lax.rem(me_y + 1, fy_count), lax.rem(me_y + fy_count - 1, fy_count)
    right, left = lax.rem(me_x + 1, fx_count), lax.rem(me_x + fx_count - 1, fx_count)

    loads = []
    for at, (source, target) in enumerate([(margin_hbm, margin), (basis_hbm, basis), (fwd_hbm, fwd_raw), (bwd_hbm, bwd_raw), (col_hbm, col)]):
        loads.append(pltpu.make_async_copy(source, target, load_sem.at[at]))
    quarters = []
    for part in range(4):
        chans = pl.ds(4 * part, 4)
        quarters.append([])
        for at, (source, target) in enumerate([(start_hbm, start), (dirty_hbm, dirty), (samp_hbm, samp)]):
            copy = pltpu.make_async_copy(source.at[chans], target.at[chans], input_sem.at[part, at])
            copy.start()
            quarters[part].append(copy)

    barrier = pltpu.get_barrier_semaphore()

    def greet(device):
        pl.semaphore_signal(barrier, inc=1, device_id=device, device_id_type=MESH)

    row, chip, core = me_y // 8, lax.rem(me_y // 2, 4), lax.rem(me_y, 2)
    plane = []
    for far in (4, 3, 2, 1, 0):
        for dy in range(4):
            for dx in range(4):
                for dc in range(2):
                    if min(dy, 4 - dy) + min(dx, 4 - dx) == far and (dy, dx, dc) != (0, 0, 0):
                        at = 8 * lax.rem(row + dy, 4) + 2 * lax.rem(chip + dx, 4) + lax.rem(core + dc, 2)
                        plane.append({"fy": at, "fx": me_x})
    line = {}
    for k in range(1, fx_count):
        line[k] = {"fy": me_y, "fx": lax.rem(me_x + k, fx_count)}
    order = sorted(line, key=lambda k: -min(k, fx_count - k))
    is_early, is_late = me_x < EARLY, me_x >= EARLY
    has_left, has_right = me_x > 0, me_x < fx_count - 1

    far0 = fx_count // 2 - 1
    is_far = jnp.logical_and(me_x >= far0, me_x < far0 + FAR)
    is_first = jnp.logical_and(me_x == 0, me_y == FIRST)

    def greet_far():
        for z in range(far0, far0 + FAR):
            def each(k, carry, z=z):
                greet({"fy": lax.rem(me_y + k, fy_count), "fx": z})
                return carry

            lax.fori_loop(1, fy_count, each, 0)

    def greet_many():
        for k in order:
            greet(line[k])
        for device in plane:
            greet(device)

    def greet_few():
        greet({"fy": over, "fx": me_x})
        greet({"fy": below, "fx": me_x})
        greet({"fy": me_y, "fx": left})

    pl.when(is_early)(greet_many)
    pl.when(is_first)(greet_far)
    pl.when(is_late)(greet_few)
    pl.when(jnp.logical_and(is_late, has_right))(lambda: greet({"fy": me_y, "fx": right}))
    pl.when(has_right)(lambda: greet({"fy": below, "fx": right}))
    pl.when(has_left)(lambda: greet({"fy": over, "fx": left}))

    lane = lax.broadcasted_iota(jnp.int32, (1, COLS), 1)
    block = lane // PAD

    energy = jnp.zeros((ROWS, COLS), F32)
    for c in range(CHANNELS):
        if c % 4 == 0:
            for copy in quarters[c // 4]:
                copy.wait()
        value = DUAL_STEP * samp[c] * start[c] - DUAL_STEP * dirty[c]
        shifted_ref[c] = value
        energy = energy + value * value
    energy = jnp.sum(energy, axis=0, keepdims=True)
    line_out[...] = energy

    one = lambda flag: flag.astype(jnp.int32)
    guests = jnp.where(
        is_early,
        len(plane) + EARLY - 1 + one(me_x == EARLY - 1) + one(has_left) + 1,
        2 + EARLY + one(me_x > EARLY) + 1 + 2 * one(has_right) + one(jnp.logical_and(is_far, me_y != FIRST)))
    pl.semaphore_wait(barrier, guests)

    def line_copy(z):
        return pltpu.make_async_remote_copy(
            src_ref=line_out, dst_ref=line_in.at[me_x], send_sem=line_sem.at[0], recv_sem=line_sem.at[1 + one(is_far)],
            device_id={"fy": me_y, "fx": z}, device_id_type=MESH)

    direct = pltpu.make_async_remote_copy(
        src_ref=line_out, dst_ref=direct_in.at[lax.rem(me_x, FAR) * fy_count + me_y], send_sem=direct_sem.at[0],
        recv_sem=direct_sem.at[1], device_id={"fy": FIRST, "fx": 0}, device_id_type=MESH)
    pl.when(is_far)(direct.start)
    for z in range(EARLY):
        pl.when(me_x != z)(lambda z=z: line_copy(z).start())

    for copy in loads:
        copy.start()
    for g in range(GROUPS):
        total = jnp.zeros((ROWS, COLS), F32)
        for q in range(4):
            value = start[4 * g + q]
            moved = value if q == 3 else pltpu.roll(value, PAD * (q + 1), 1)
            total = jnp.where(block == q, moved, total)
        pack[g] = total

    halos = []
    for h in range(HALVES):
        chans = pl.ds(h * PER, PER)
        groups = pl.ds(h * PER // 4, PER // 4)
        for at, (source, target, device) in enumerate([
            (start.at[chans], above.at[chans], {"fy": below, "fx": me_x}),
            (pack.at[groups], left_in.at[groups], {"fy": me_y, "fx": right}),
            (pack.at[groups], corner_in.at[groups], {"fy": below, "fx": right}),
        ]):
            copy = pltpu.make_async_remote_copy(
                src_ref=source, dst_ref=target, send_sem=halo_send.at[h, at], recv_sem=halo_recv.at[h, at],
                device_id=device, device_id_type=MESH)
            if at == 0:
                copy.start()
            else:
                pl.when(has_right)(copy.start)
            halos.append(copy)

    def no_left():
        left_in[...] = jnp.zeros_like(left_in)
        corner_in[...] = jnp.zeros_like(corner_in)

    def no_right():
        left_back[...] = jnp.zeros_like(left_back)
        corner_back[...] = jnp.zeros_like(corner_back)

    pl.when(jnp.logical_not(has_left))(no_left)
    pl.when(jnp.logical_not(has_right))(no_right)

    for copy in loads:
        copy.wait()
    row_has = (me_y > 0).astype(jnp.int32)
    col_has = (me_x > 0).astype(jnp.int32)
    keep_rows = [margin[0, 0, l, 0] * row_has for l in range(LEVELS)]
    keep_cols = [margin[0, 0, l, 1] * col_has for l in range(LEVELS)]

    row_at = lax.broadcasted_iota(jnp.int32, (128, 192), 0)
    col_at = lax.rem(lax.broadcasted_iota(jnp.int32, (128, 192), 1), 64)
    reach = jnp.where(row_at < 64, keep_rows[0], keep_rows[1])
    fwd_m[...] = jnp.where(PAD - col_at <= reach, fwd_raw[...], 0.0).astype(BF)
    row_at = lax.broadcasted_iota(jnp.int32, (64, 384), 0)
    col_at = lax.rem(lax.broadcasted_iota(jnp.int32, (64, 384), 1), 128)
    reach = jnp.where(col_at < 64, keep_rows[0], keep_rows[1])
    bwd_m[...] = jnp.where(PAD - row_at <= reach, bwd_raw[...], 0.0).astype(BF)

    kept = []
    for l in range(LEVELS):
        inside = PAD - lax.rem(lane, PAD) <= keep_cols[l]
        kept.append([jnp.logical_and(inside, block == q) for q in range(4)])

    columns = []
    diagonal = lax.broadcasted_iota(jnp.int32, (CHANNELS, CHANNELS), 0) == lax.broadcasted_iota(jnp.int32, (CHANNELS, CHANNELS), 1)
    for r in range(RANK):
        vector = jnp.sum(jnp.where(diagonal, basis[r : r + 1, :], 0.0), axis=1, keepdims=True)
        vector = jnp.broadcast_to(vector, (CHANNELS, COLS))
        for previous in columns:
            vector = vector - jnp.sum(previous * vector, axis=0, keepdims=True) * previous
        vector = vector / jnp.sqrt(jnp.sum(vector * vector, axis=0, keepdims=True))
        columns.append(vector)
        spec[r] = vector

    def project(field):
        weights = []
        for r in range(RANK):
            total = spec[r, 0:1, :] * field(0)
            for c in range(1, CHANNELS):
                total = total + spec[r, c : c + 1, :] * field(c)
            weights.append(total)

        def channel(c):
            total = spec[0, c : c + 1, :] * weights[0]
            for r in range(1, RANK):
                total = total + spec[r, c : c + 1, :] * weights[r]
            return total

        return channel

    pb = project(lambda c: PRIMAL_STEP * samp[c] * shifted_ref[c])
    for c in range(CHANNELS):
        pb_ref[c] = pb(c)

    def place(target, p, part, row0, value):
        high, low = split(value)
        lanes = pl.ds(COLS * part, COLS)
        target[p, pl.ds(row0, ROWS), lanes] = high
        target[p, pl.ds(64 + row0, ROWS), lanes] = low
        target[p, pl.ds(128 + row0, ROWS), lanes] = high

    for c in range(CHANNELS):
        place(x_own, c // 2, c % 2, PAD, start[c])

    backs = []
    for h in range(HALVES):
        halos[3 * h].wait_recv()

        def from_left(h=h):
            halos[3 * h + 1].wait_recv()
            halos[3 * h + 2].wait_recv()

        pl.when(has_left)(from_left)
        first = h * PER
        for c in range(first, first + PER):
            place(x_own, c // 2, c % 2, 0, above[c])
        for g in range(first // 4, (first + PER) // 4):
            place(x_left, g, 0, 0, corner_in[g])
            place(x_left, g, 0, PAD, left_in[g])
        for p in range(first // 2, (first + PER) // 2):
            u = dot(fwd_m[...], x_own[p])
            high, low = split(u)
            for part in range(2):
                c = 2 * p + part - first
                lanes = slice(COLS * part, COLS * (part + 1))
                for l in range(LEVELS):
                    lhs[l, pl.ds(64 * c, 64), 0:128] = high[64 * l : 64 * l + 64, lanes]
                    lhs[l, pl.ds(64 * c, 64), 256:384] = low[64 * l : 64 * l + 64, lanes]
        for g in range(first // 4, (first + PER) // 4):
            u = dot(fwd_m[...], x_left[g])
            for q in range(4):
                c = 4 * g + q - first
                for l in range(LEVELS):
                    high, low = split(jnp.where(kept[l][q], u[64 * l : 64 * l + 64, :], 0.0))
                    lhs[l, pl.ds(64 * c, 64), 128:256] = high
                    lhs[l, pl.ds(64 * c, 64), 384:512] = low
        z_sum = [[jnp.zeros((64, COLS), F32) for l in range(LEVELS)] for g in range(PER // 4)]
        for l in range(LEVELS):
            acc = dot(lhs[l, :, 0:256], col[l]) + dot(lhs[l, :, 256:512], col[l])
            acc = jnp.clip(acc, -CLIP_LEVEL, CLIP_LEVEL)
            high, low = split(acc)
            for c in range(PER):
                zero = jnp.zeros((32, COLS), BF)
                top, mid, end = 64 * c, 64 * c + 32, 64 * c + 64
                bands[pl.ds(top, 32), 0:128] = zero
                bands[pl.ds(top, 32), 256:384] = zero
                bands[pl.ds(top, 32), 128:256] = high[top:mid, 128:256]
                bands[pl.ds(top, 32), 384:512] = low[top:mid, 128:256]
                bands[pl.ds(mid, 32), 0:256] = high[mid:end, :]
                bands[pl.ds(mid, 32), 256:512] = low[mid:end, :]
            z = dot(bands[:, 0:256], col[LEVELS + l]) + dot(bands[:, 256:512], col[LEVELS + l])
            for c in range(PER):
                high, low = split(z[64 * c : 64 * c + 64, 0:128])
                lanes = pl.ds(COLS * (c % 2), COLS)
                z_own[c // 2, pl.ds(64 * l, 64), lanes] = high
                z_own[c // 2, pl.ds(128 + 64 * l, 64), lanes] = low
                piece = z[64 * c : 64 * c + 64, 128:256]
                z_sum[c // 4][l] = z_sum[c // 4][l] + jnp.where(kept[l][c % 4], piece, 0.0)
        for g in range(PER // 4):
            for l in range(LEVELS):
                high, low = split(z_sum[g][l])
                z_left[g, pl.ds(64 * l, 64), :] = high
                z_left[g, pl.ds(128 + 64 * l, 64), :] = low
            left_out[first // 4 + g] = dot(bwd_m[:, 0:256], z_left[g]) + dot(bwd_m[:, 256:384], z_left[g, 0:128, :])
        for p in range(PER // 2):
            r = dot(bwd_m[:, 0:256], z_own[p]) + dot(bwd_m[:, 256:384], z_own[p, 0:128, :])
            for part in range(2):
                c = first + 2 * p + part
                up_out[c] = r[0:32, COLS * part : COLS * (part + 1)]
                own[c] = r[32:64, COLS * part : COLS * (part + 1)]
        chans = pl.ds(first, PER)
        groups = pl.ds(first // 4, PER // 4)
        for at, (source, target, device) in enumerate([
            (left_out.at[groups, pl.ds(32, 32), :], left_back.at[groups], {"fy": me_y, "fx": left}),
            (left_out.at[groups, pl.ds(0, 32), :], corner_back.at[groups], {"fy": over, "fx": left}),
            (up_out.at[chans], up_in.at[chans], {"fy": over, "fx": me_x}),
        ]):
            copy = pltpu.make_async_remote_copy(
                src_ref=source, dst_ref=target, send_sem=back_send.at[h, at], recv_sem=back_recv.at[h, at],
                device_id=device, device_id_type=MESH)
            if at == 2:
                copy.start()
            else:
                pl.when(has_left)(copy.start)
            backs.append(copy)

    def arrived(ref, count, sem):
        pltpu.make_async_copy(ref.at[pl.ds(0, count)], ref.at[pl.ds(0, count)], sem).wait()

    def plane_copy(source, device):
        return pltpu.make_async_remote_copy(
            src_ref=source, dst_ref=plane_in.at[me_y], send_sem=plane_sem.at[0], recv_sem=plane_sem.at[1],
            device_id=device, device_id_type=MESH)

    def exchange():
        arrived(line_in, fx_count - 1 - FAR, line_sem.at[1])
        line_in[me_x] = line_out[...]
        side = jnp.sum(line_in[0:far0], axis=0) + jnp.sum(line_in[far0 + FAR :], axis=0)
        side_out[...] = side
        plane_in[me_y] = side
        pl.when(jnp.logical_and(me_x == 0, me_y != FIRST))(plane_copy(side_out, {"fy": FIRST, "fx": 0}).start)
        arrived(line_in, FAR, line_sem.at[2])
        whole = side_out[...] + jnp.sum(line_in[far0 : far0 + FAR], axis=0)
        plane_out[...] = whole

        def keep_whole():
            plane_in[me_y] = whole

        pl.when(jnp.logical_not(is_first))(keep_whole)
        for device in plane:
            pl.when(jnp.logical_or(me_x != 0, device["fy"] != FIRST))(plane_copy(plane_out, device).start)

    pl.when(is_early)(exchange)

    for at, copy in enumerate(backs):
        if at % 3 == 2:
            copy.wait_recv()
        else:
            pl.when(has_right)(copy.wait_recv)
    for g in range(GROUPS):
        strip = left_back[g] + corner_back[g]
        for q in range(4):
            c = 4 * g + q
            moved = strip if q == 3 else pltpu.roll(strip, COLS - PAD * (q + 1), 1)
            own[c] = start[c] - (own[c] + up_in[c] + jnp.where(block == 3, moved, 0.0))
    pa = project(lambda c: own[c])
    for c in range(CHANNELS):
        pa_ref[c] = pa(c)

    def total_copy(z):
        return pltpu.make_async_remote_copy(
            src_ref=total_out, dst_ref=total_in, send_sem=total_sem.at[0], recv_sem=total_sem.at[1],
            device_id={"fy": me_y, "fx": z}, device_id_type=MESH)

    shares = {EARLY - 1: sorted(range(EARLY, fx_count), key=lambda z: abs(z - EARLY + 1 - fx_count // 2))}

    def finish():
        arrived(plane_in, fy_count - 1, plane_sem.at[1])
        total = jnp.sum(plane_in[...], axis=0)
        total_in[...] = total
        total_out[...] = total

    def add_far():
        arrived(direct_in, FAR * fy_count, direct_sem.at[1])
        total_in[...] = total_in[...] + jnp.sum(direct_in[...], axis=0)

    def hand(zs):
        for z in zs:
            total_copy(z).start()

    for at, copy in enumerate(halos):
        if at % 3 == 0:
            copy.wait_send()
        else:
            pl.when(has_right)(copy.wait_send)
    for at, copy in enumerate(backs):
        if at % 3 == 2:
            copy.wait_send()
        else:
            pl.when(has_left)(copy.wait_send)

    def early_sent():
        arrived(line_in, EARLY - 1, line_sem.at[0])
        arrived(plane_in, fy_count - 1, plane_sem.at[0])

    pl.when(is_early)(early_sent)
    pl.when(is_late)(lambda: arrived(line_in, EARLY, line_sem.at[0]))
    pl.when(is_far)(direct.wait_send)

    pl.when(is_early)(finish)
    pl.when(is_first)(add_far)
    pl.when(is_late)(lambda: total_copy(0).wait_recv())
    total = jnp.sum(total_in[...], axis=1, keepdims=True)
    radius = BALL_SCALE * math.sqrt(CHANNELS * ROWS * COLS * fy_count * fx_count)
    factor = jnp.maximum(0.0, 1.0 - DUAL_STEP * radius / jnp.sqrt(total + NORM_EPS))
    factor_ref[...] = jnp.broadcast_to(factor, (1, COLS))

    for z, zs in shares.items():
        pl.when(me_x == z)(functools.partial(hand, zs))
    for z, zs in shares.items():
        pl.when(me_x == z)(functools.partial(arrived, line_in, len(zs), total_sem.at[0]))


def last_step(pa_ref, pb_ref, shifted_ref, factor_ref, image_hbm, dual_hbm, image, dual, sems):
    factor = factor_ref[...]
    copies = []
    for part in range(4):
        for c in range(4 * part, 4 * part + 4):
            image[c] = jnp.maximum(pa_ref[c] - factor * pb_ref[c], 0.0)
            dual[c] = factor * shifted_ref[c]
        chans = pl.ds(4 * part, 4)
        for at, (source, target) in enumerate([(image, image_hbm), (dual, dual_hbm)]):
            copy = pltpu.make_async_copy(source.at[chans], target.at[chans], sems.at[part, at])
            copy.start()
            copies.append(copy)
    for copy in copies:
        copy.wait()


def per_device(fy_count, fx_count, start_image, dirty, sampling, basis_seed, margin):
    forward, backward, column = tables()
    tile = jax.ShapeDtypeStruct((CHANNELS, ROWS, COLS), F32)
    hbm = pl.BlockSpec(memory_space=pltpu.HBM)
    vmem = pl.BlockSpec(memory_space=pltpu.VMEM)
    field = pltpu.VMEM((CHANNELS, ROWS, COLS), F32)
    strips = pltpu.VMEM((GROUPS, ROWS, COLS), F32)
    dma = pltpu.SemaphoreType.DMA

    def body(*refs):
        kernel_body(fy_count, fx_count, *refs)

    pa, pb, shifted, factor = pl.pallas_call(
        body,
        out_shape=(tile, tile, tile, jax.ShapeDtypeStruct((1, COLS), F32)),
        in_specs=[hbm] * 8,
        out_specs=(vmem,) * 4,
        scratch_shapes=[
            field, field, field,
            pltpu.VMEM((RANK, CHANNELS), F32),
            pltpu.SMEM((1, 1, LEVELS, 2), jnp.int32),
            pltpu.VMEM((128, 192), F32), pltpu.VMEM((64, 384), F32), pltpu.VMEM((2 * LEVELS, 256, 256), BF),
            pltpu.VMEM((128, 192), BF), pltpu.VMEM((64, 384), BF),
            strips, field, strips, strips,
            pltpu.VMEM((CHANNELS // 2, 192, 256), BF), pltpu.VMEM((GROUPS, 192, COLS), BF),
            pltpu.VMEM((LEVELS, 64 * PER, 512), BF), pltpu.VMEM((64 * PER, 512), BF),
            pltpu.VMEM((PER // 2, 256, 256), BF), pltpu.VMEM((PER // 4, 256, COLS), BF),
            field, field, pltpu.VMEM((GROUPS, 64, COLS), F32), field, strips, strips,
            pltpu.VMEM((RANK, CHANNELS, COLS), F32),
            pltpu.VMEM((1, COLS), F32), pltpu.VMEM((fx_count, 1, COLS), F32),
            pltpu.VMEM((1, COLS), F32), pltpu.VMEM((fy_count, 1, COLS), F32),
            pltpu.VMEM((1, COLS), F32), pltpu.VMEM((FAR * fy_count, 1, COLS), F32),
            pltpu.VMEM((1, COLS), F32), pltpu.VMEM((1, COLS), F32),
            dma((4, 3)), dma((5,)), dma((HALVES, 3)), dma((HALVES, 3)), dma((3,)), dma((2,)), dma((2,)), dma((2,)), dma((HALVES, 3)), dma((HALVES, 3)),
        ],
        compiler_params=pltpu.CompilerParams(collective_id=0, has_side_effects=True, vmem_limit_bytes=40 * 1024 * 1024),
        name="step",
    )(*(pltpu.with_memory_space_constraint(value, pltpu.HBM) for value in (
        start_image, dirty, sampling, basis_seed.T, margin,
        jnp.asarray(forward, F32), jnp.asarray(backward, F32), jnp.asarray(column, BF))))
    return pl.pallas_call(
        last_step,
        out_shape=(tile, tile),
        in_specs=[vmem] * 4,
        out_specs=(hbm, hbm),
        scratch_shapes=[field, field, dma((4, 2))],
        compiler_params=pltpu.CompilerParams(vmem_limit_bytes=4 * 1024 * 1024),
        name="last",
    )(pa, pb, shifted, factor)


def solution(mesh):
    fy_count, fx_count = mesh.shape["fy"], mesh.shape["fx"]

    def step(*args):
        return per_device(fy_count, fx_count, *args)

    image = P(None, "fy", "fx")
    return jax.shard_map(
        step, mesh=mesh, in_specs=(image, image, image, P(), P("fy", "fx", None, None)),
        out_specs=(image, image), check_vma=False)
```

```python
import functools
import math

import jax
import jax.numpy as jnp
import numpy as np
from jax import lax
from jax.experimental import pallas as pl
from jax.experimental.pallas import tpu as pltpu
from jax.sharding import PartitionSpec as P

MESH = pl.DeviceIdType.MESH
BF = jnp.bfloat16
F32 = jnp.float32

LEVELS = 2
PAD = 32
ROWS = 32
COLS = 128
CHANNELS = 16
RANK = 4
HALVES = 2
EARLY = 4
FIRST = 1
FAR = 6
PER = CHANNELS // HALVES
GROUPS = CHANNELS // 4


DAUBECHIES = [
    -0.00011747678400228192,
    0.0006754494059985568,
    -0.0003917403729959771,
    -0.00487035299301066,
    0.008746094047015655,
    0.013981027917015516,
    -0.04408825393106472,
    -0.01736930100202211,
    0.128747426620186,
    0.00047248457399797254,
    -0.2840155429624281,
    -0.015829105256023893,
    0.5853546836548691,
    0.6756307362980128,
    0.3128715909144659,
    0.05441584224308161,
]
DUAL_STEP = 0.5
PRIMAL_STEP = 0.5
CLIP_LEVEL = 0.08
BALL_SCALE = 0.8
NORM_EPS = 1e-06


def taps_pair():
    low = [tap / math.sqrt(2.0) for tap in DAUBECHIES]
    high = [(-1.0) ** k * low[len(low) - 1 - k] for k in range(len(low))]
    return low, high


def band_matrix(taps, extent, dilation):
    matrix = np.zeros((extent + PAD, extent), np.float64)
    for k, tap in enumerate(taps):
        for i in range(extent):
            matrix[i + PAD - k * dilation, i] += tap
    return matrix


def split_host(matrix):
    high = matrix.astype(np.float32).astype(jnp.bfloat16)
    low = (matrix - high.astype(np.float64)).astype(np.float32).astype(jnp.bfloat16)
    return high, low


def tables():
    low, high = taps_pair()
    scale = DUAL_STEP / math.sqrt(LEVELS)
    rows, cols = [], []
    for level in range(LEVELS):
        d = 2**level
        rows.append(band_matrix(low, ROWS, d).T)
        rows.append(band_matrix(high, ROWS, d).T)
        both = np.concatenate([band_matrix(low, COLS, d), band_matrix(high, COLS, d)], axis=1) * scale
        cols.append(np.concatenate([both[PAD:]] + [both[:PAD]] * 4, axis=0))
    row_all = np.concatenate(rows, axis=0)
    hi, lo = (part.astype(np.float32) for part in split_host(row_all))
    forward = np.concatenate([hi, hi, lo], axis=1)
    backward = np.concatenate([hi.T, hi.T, lo.T], axis=1)
    column = []
    for level in range(LEVELS):
        column.extend(split_host(cols[level]))
    for level in range(LEVELS):
        column.extend(split_host(cols[level].T))
    return forward, backward, np.stack(column)


def split(value):
    high = value.astype(BF)
    return high, (value - high.astype(F32)).astype(BF)


def dot(a, b):
    return jnp.dot(a, b, preferred_element_type=F32)


def kernel_body(fy_count, fx_count, start_hbm, dirty_hbm, samp_hbm, basis_hbm, margin_hbm, fwd_hbm, bwd_hbm, col_hbm,
                pa_ref, pb_ref, shifted_ref, factor_ref,
                start, dirty, samp, basis, margin, fwd_raw, bwd_raw, col,
                fwd_m, bwd_m, pack, above, left_in, corner_in,
                x_own, x_left, lhs, bands, z_own, z_left, own, up_out, left_out, up_in, left_back, corner_back,
                spec, line_out, line_in, plane_out, plane_in, side_out, direct_in, total_out, total_in,
                input_sem, load_sem, halo_send, halo_recv, line_sem, plane_sem, direct_sem, total_sem, back_send, back_recv):
    me_y, me_x = lax.axis_index("fy"), lax.axis_index("fx")
    below, over = lax.rem(me_y + 1, fy_count), lax.rem(me_y + fy_count - 1, fy_count)
    right, left = lax.rem(me_x + 1, fx_count), lax.rem(me_x + fx_count - 1, fx_count)

    loads = []
    for at, (source, target) in enumerate([(margin_hbm, margin), (basis_hbm, basis), (fwd_hbm, fwd_raw), (bwd_hbm, bwd_raw), (col_hbm, col)]):
        loads.append(pltpu.make_async_copy(source, target, load_sem.at[at]))
    quarters = []
    for part in range(4):
        chans = pl.ds(4 * part, 4)
        quarters.append([])
        for at, (source, target) in enumerate([(start_hbm, start), (dirty_hbm, dirty), (samp_hbm, samp)]):
            copy = pltpu.make_async_copy(source.at[chans], target.at[chans], input_sem.at[part, at])
            copy.start()
            quarters[part].append(copy)

    barrier = pltpu.get_barrier_semaphore()

    def greet(device):
        pl.semaphore_signal(barrier, inc=1, device_id=device, device_id_type=MESH)

    row, chip, core = me_y // 8, lax.rem(me_y // 2, 4), lax.rem(me_y, 2)
    plane = []
    for far in (4, 3, 2, 1, 0):
        for dy in range(4):
            for dx in range(4):
                for dc in range(2):
                    if min(dy, 4 - dy) + min(dx, 4 - dx) == far and (dy, dx, dc) != (0, 0, 0):
                        at = 8 * lax.rem(row + dy, 4) + 2 * lax.rem(chip + dx, 4) + lax.rem(core + dc, 2)
                        plane.append({"fy": at, "fx": me_x})
    line = {}
    for k in range(1, fx_count):
        line[k] = {"fy": me_y, "fx": lax.rem(me_x + k, fx_count)}
    order = sorted(line, key=lambda k: -min(k, fx_count - k))
    is_early, is_late = me_x < EARLY, me_x >= EARLY
    has_left, has_right = me_x > 0, me_x < fx_count - 1

    far0 = fx_count // 2 - 2
    is_far = jnp.logical_and(me_x >= far0, me_x < far0 + FAR)
    is_first = jnp.logical_and(me_x == 0, me_y == FIRST)

    def greet_far():
        for z in range(far0, far0 + FAR):
            def each(k, carry, z=z):
                greet({"fy": lax.rem(me_y + k, fy_count), "fx": z})
                return carry

            lax.fori_loop(1, fy_count, each, 0)

    def greet_many():
        for k in order:
            greet(line[k])
        for device in plane:
            greet(device)

    def greet_few():
        greet({"fy": over, "fx": me_x})
        greet({"fy": below, "fx": me_x})
        greet({"fy": me_y, "fx": left})

    pl.when(is_early)(greet_many)
    pl.when(is_first)(greet_far)
    pl.when(is_late)(greet_few)
    pl.when(jnp.logical_and(is_late, has_right))(lambda: greet({"fy": me_y, "fx": right}))
    pl.when(has_right)(lambda: greet({"fy": below, "fx": right}))
    pl.when(has_left)(lambda: greet({"fy": over, "fx": left}))

    lane = lax.broadcasted_iota(jnp.int32, (1, COLS), 1)
    block = lane // PAD

    energy = jnp.zeros((ROWS, COLS), F32)
    for c in range(CHANNELS):
        if c % 4 == 0:
            for copy in quarters[c // 4]:
                copy.wait()
        value = DUAL_STEP * samp[c] * start[c] - DUAL_STEP * dirty[c]
        shifted_ref[c] = value
        energy = energy + value * value
    energy = jnp.sum(energy, axis=0, keepdims=True)
    line_out[...] = energy

    one = lambda flag: flag.astype(jnp.int32)
    guests = jnp.where(
        is_early,
        len(plane) + EARLY - 1 + one(me_x == EARLY - 1) + one(has_left) + 1,
        2 + EARLY + one(me_x > EARLY) + 1 + 2 * one(has_right) + one(jnp.logical_and(is_far, me_y != FIRST)))
    pl.semaphore_wait(barrier, guests)

    def line_copy(z):
        return pltpu.make_async_remote_copy(
            src_ref=line_out, dst_ref=line_in.at[me_x], send_sem=line_sem.at[0], recv_sem=line_sem.at[1 + one(is_far)],
            device_id={"fy": me_y, "fx": z}, device_id_type=MESH)

    direct = pltpu.make_async_remote_copy(
        src_ref=line_out, dst_ref=direct_in.at[lax.rem(me_x, FAR) * fy_count + me_y], send_sem=direct_sem.at[0],
        recv_sem=direct_sem.at[1], device_id={"fy": FIRST, "fx": 0}, device_id_type=MESH)
    pl.when(is_far)(direct.start)
    for z in range(EARLY):
        pl.when(me_x != z)(lambda z=z: line_copy(z).start())

    for copy in loads:
        copy.start()
    for g in range(GROUPS):
        total = jnp.zeros((ROWS, COLS), F32)
        for q in range(4):
            value = start[4 * g + q]
            moved = value if q == 3 else pltpu.roll(value, PAD * (q + 1), 1)
            total = jnp.where(block == q, moved, total)
        pack[g] = total

    halos = []
    for h in range(HALVES):
        chans = pl.ds(h * PER, PER)
        groups = pl.ds(h * PER // 4, PER // 4)
        for at, (source, target, device) in enumerate([
            (start.at[chans], above.at[chans], {"fy": below, "fx": me_x}),
            (pack.at[groups], left_in.at[groups], {"fy": me_y, "fx": right}),
            (pack.at[groups], corner_in.at[groups], {"fy": below, "fx": right}),
        ]):
            copy = pltpu.make_async_remote_copy(
                src_ref=source, dst_ref=target, send_sem=halo_send.at[h, at], recv_sem=halo_recv.at[h, at],
                device_id=device, device_id_type=MESH)
            if at == 0:
                copy.start()
            else:
                pl.when(has_right)(copy.start)
            halos.append(copy)

    def no_left():
        left_in[...] = jnp.zeros_like(left_in)
        corner_in[...] = jnp.zeros_like(corner_in)

    def no_right():
        left_back[...] = jnp.zeros_like(left_back)
        corner_back[...] = jnp.zeros_like(corner_back)

    pl.when(jnp.logical_not(has_left))(no_left)
    pl.when(jnp.logical_not(has_right))(no_right)

    for copy in loads:
        copy.wait()
    row_has = (me_y > 0).astype(jnp.int32)
    col_has = (me_x > 0).astype(jnp.int32)
    keep_rows = [margin[0, 0, l, 0] * row_has for l in range(LEVELS)]
    keep_cols = [margin[0, 0, l, 1] * col_has for l in range(LEVELS)]

    row_at = lax.broadcasted_iota(jnp.int32, (128, 192), 0)
    col_at = lax.rem(lax.broadcasted_iota(jnp.int32, (128, 192), 1), 64)
    reach = jnp.where(row_at < 64, keep_rows[0], keep_rows[1])
    fwd_m[...] = jnp.where(PAD - col_at <= reach, fwd_raw[...], 0.0).astype(BF)
    row_at = lax.broadcasted_iota(jnp.int32, (64, 384), 0)
    col_at = lax.rem(lax.broadcasted_iota(jnp.int32, (64, 384), 1), 128)
    reach = jnp.where(col_at < 64, keep_rows[0], keep_rows[1])
    bwd_m[...] = jnp.where(PAD - row_at <= reach, bwd_raw[...], 0.0).astype(BF)

    kept = []
    for l in range(LEVELS):
        inside = PAD - lax.rem(lane, PAD) <= keep_cols[l]
        kept.append([jnp.logical_and(inside, block == q) for q in range(4)])

    columns = []
    diagonal = lax.broadcasted_iota(jnp.int32, (CHANNELS, CHANNELS), 0) == lax.broadcasted_iota(jnp.int32, (CHANNELS, CHANNELS), 1)
    for r in range(RANK):
        vector = jnp.sum(jnp.where(diagonal, basis[r : r + 1, :], 0.0), axis=1, keepdims=True)
        vector = jnp.broadcast_to(vector, (CHANNELS, COLS))
        for previous in columns:
            vector = vector - jnp.sum(previous * vector, axis=0, keepdims=True) * previous
        vector = vector / jnp.sqrt(jnp.sum(vector * vector, axis=0, keepdims=True))
        columns.append(vector)
        spec[r] = vector

    def project(field):
        weights = []
        for r in range(RANK):
            total = spec[r, 0:1, :] * field(0)
            for c in range(1, CHANNELS):
                total = total + spec[r, c : c + 1, :] * field(c)
            weights.append(total)

        def channel(c):
            total = spec[0, c : c + 1, :] * weights[0]
            for r in range(1, RANK):
                total = total + spec[r, c : c + 1, :] * weights[r]
            return total

        return channel

    pb = project(lambda c: PRIMAL_STEP * samp[c] * shifted_ref[c])
    for c in range(CHANNELS):
        pb_ref[c] = pb(c)

    def place(target, p, part, row0, value):
        high, low = split(value)
        lanes = pl.ds(COLS * part, COLS)
        target[p, pl.ds(row0, ROWS), lanes] = high
        target[p, pl.ds(64 + row0, ROWS), lanes] = low
        target[p, pl.ds(128 + row0, ROWS), lanes] = high

    for c in range(CHANNELS):
        place(x_own, c // 2, c % 2, PAD, start[c])

    backs = []
    for h in range(HALVES):
        halos[3 * h].wait_recv()

        def from_left(h=h):
            halos[3 * h + 1].wait_recv()
            halos[3 * h + 2].wait_recv()

        pl.when(has_left)(from_left)
        first = h * PER
        for c in range(first, first + PER):
            place(x_own, c // 2, c % 2, 0, above[c])
        for g in range(first // 4, (first + PER) // 4):
            place(x_left, g, 0, 0, corner_in[g])
            place(x_left, g, 0, PAD, left_in[g])
        for p in range(first // 2, (first + PER) // 2):
            u = dot(fwd_m[...], x_own[p])
            high, low = split(u)
            for part in range(2):
                c = 2 * p + part - first
                lanes = slice(COLS * part, COLS * (part + 1))
                for l in range(LEVELS):
                    lhs[l, pl.ds(64 * c, 64), 0:128] = high[64 * l : 64 * l + 64, lanes]
                    lhs[l, pl.ds(64 * c, 64), 256:384] = low[64 * l : 64 * l + 64, lanes]
        for g in range(first // 4, (first + PER) // 4):
            u = dot(fwd_m[...], x_left[g])
            for q in range(4):
                c = 4 * g + q - first
                for l in range(LEVELS):
                    high, low = split(jnp.where(kept[l][q], u[64 * l : 64 * l + 64, :], 0.0))
                    lhs[l, pl.ds(64 * c, 64), 128:256] = high
                    lhs[l, pl.ds(64 * c, 64), 384:512] = low
        z_sum = [[jnp.zeros((64, COLS), F32) for l in range(LEVELS)] for g in range(PER // 4)]
        for l in range(LEVELS):
            acc = dot(lhs[l, :, 0:256], col[2 * l]) + dot(lhs[l, :, 256:512], col[2 * l]) + dot(lhs[l, :, 0:256], col[2 * l + 1])
            acc = jnp.clip(acc, -CLIP_LEVEL, CLIP_LEVEL)
            high, low = split(acc)
            for c in range(PER):
                zero = jnp.zeros((32, COLS), BF)
                top, mid, end = 64 * c, 64 * c + 32, 64 * c + 64
                bands[pl.ds(top, 32), 0:128] = zero
                bands[pl.ds(top, 32), 256:384] = zero
                bands[pl.ds(top, 32), 128:256] = high[top:mid, 128:256]
                bands[pl.ds(top, 32), 384:512] = low[top:mid, 128:256]
                bands[pl.ds(mid, 32), 0:256] = high[mid:end, :]
                bands[pl.ds(mid, 32), 256:512] = low[mid:end, :]
            at = 2 * LEVELS + 2 * l
            z = dot(bands[:, 0:256], col[at]) + dot(bands[:, 256:512], col[at]) + dot(bands[:, 0:256], col[at + 1])
            for c in range(PER):
                high, low = split(z[64 * c : 64 * c + 64, 0:128])
                lanes = pl.ds(COLS * (c % 2), COLS)
                z_own[c // 2, pl.ds(64 * l, 64), lanes] = high
                z_own[c // 2, pl.ds(128 + 64 * l, 64), lanes] = low
                piece = z[64 * c : 64 * c + 64, 128:256]
                z_sum[c // 4][l] = z_sum[c // 4][l] + jnp.where(kept[l][c % 4], piece, 0.0)
        for g in range(PER // 4):
            for l in range(LEVELS):
                high, low = split(z_sum[g][l])
                z_left[g, pl.ds(64 * l, 64), :] = high
                z_left[g, pl.ds(128 + 64 * l, 64), :] = low
            left_out[first // 4 + g] = dot(bwd_m[:, 0:256], z_left[g]) + dot(bwd_m[:, 256:384], z_left[g, 0:128, :])
        for p in range(PER // 2):
            r = dot(bwd_m[:, 0:256], z_own[p]) + dot(bwd_m[:, 256:384], z_own[p, 0:128, :])
            for part in range(2):
                c = first + 2 * p + part
                up_out[c] = r[0:32, COLS * part : COLS * (part + 1)]
                own[c] = r[32:64, COLS * part : COLS * (part + 1)]
        chans = pl.ds(first, PER)
        groups = pl.ds(first // 4, PER // 4)
        for at, (source, target, device) in enumerate([
            (left_out.at[groups, pl.ds(32, 32), :], left_back.at[groups], {"fy": me_y, "fx": left}),
            (left_out.at[groups, pl.ds(0, 32), :], corner_back.at[groups], {"fy": over, "fx": left}),
            (up_out.at[chans], up_in.at[chans], {"fy": over, "fx": me_x}),
        ]):
            copy = pltpu.make_async_remote_copy(
                src_ref=source, dst_ref=target, send_sem=back_send.at[h, at], recv_sem=back_recv.at[h, at],
                device_id=device, device_id_type=MESH)
            if at == 2:
                copy.start()
            else:
                pl.when(has_left)(copy.start)
            backs.append(copy)

    def arrived(ref, count, sem):
        pltpu.make_async_copy(ref.at[pl.ds(0, count)], ref.at[pl.ds(0, count)], sem).wait()

    def plane_copy(source, device):
        return pltpu.make_async_remote_copy(
            src_ref=source, dst_ref=plane_in.at[me_y], send_sem=plane_sem.at[0], recv_sem=plane_sem.at[1],
            device_id=device, device_id_type=MESH)

    def exchange():
        arrived(line_in, fx_count - 1 - FAR, line_sem.at[1])
        line_in[me_x] = line_out[...]
        side = jnp.sum(line_in[0:far0], axis=0) + jnp.sum(line_in[far0 + FAR :], axis=0)
        side_out[...] = side
        plane_in[me_y] = side
        pl.when(jnp.logical_and(me_x == 0, me_y != FIRST))(plane_copy(side_out, {"fy": FIRST, "fx": 0}).start)
        arrived(line_in, FAR, line_sem.at[2])
        whole = side_out[...] + jnp.sum(line_in[far0 : far0 + FAR], axis=0)
        plane_out[...] = whole

        def keep_whole():
            plane_in[me_y] = whole

        pl.when(jnp.logical_not(is_first))(keep_whole)
        for device in plane:
            pl.when(jnp.logical_or(me_x != 0, device["fy"] != FIRST))(plane_copy(plane_out, device).start)

    pl.when(is_early)(exchange)

    for at, copy in enumerate(backs):
        if at % 3 == 2:
            copy.wait_recv()
        else:
            pl.when(has_right)(copy.wait_recv)
    for g in range(GROUPS):
        strip = left_back[g] + corner_back[g]
        for q in range(4):
            c = 4 * g + q
            moved = strip if q == 3 else pltpu.roll(strip, COLS - PAD * (q + 1), 1)
            own[c] = start[c] - (own[c] + up_in[c] + jnp.where(block == 3, moved, 0.0))
    pa = project(lambda c: own[c])
    for c in range(CHANNELS):
        pa_ref[c] = pa(c)

    def total_copy(z):
        return pltpu.make_async_remote_copy(
            src_ref=total_out, dst_ref=total_in, send_sem=total_sem.at[0], recv_sem=total_sem.at[1],
            device_id={"fy": me_y, "fx": z}, device_id_type=MESH)

    shares = {EARLY - 1: sorted(range(EARLY, fx_count), key=lambda z: abs(z - EARLY + 1 - fx_count // 2))}

    def finish():
        arrived(plane_in, fy_count - 1, plane_sem.at[1])
        total = jnp.sum(plane_in[...], axis=0)
        total_in[...] = total
        total_out[...] = total

    def add_far():
        arrived(direct_in, FAR * fy_count, direct_sem.at[1])
        total_in[...] = total_in[...] + jnp.sum(direct_in[...], axis=0)

    def hand(zs):
        for z in zs:
            total_copy(z).start()

    for at, copy in enumerate(halos):
        if at % 3 == 0:
            copy.wait_send()
        else:
            pl.when(has_right)(copy.wait_send)
    for at, copy in enumerate(backs):
        if at % 3 == 2:
            copy.wait_send()
        else:
            pl.when(has_left)(copy.wait_send)

    def early_sent():
        arrived(line_in, EARLY - 1, line_sem.at[0])
        arrived(plane_in, fy_count - 1, plane_sem.at[0])

    pl.when(is_early)(early_sent)
    pl.when(is_late)(lambda: arrived(line_in, EARLY, line_sem.at[0]))
    pl.when(is_far)(direct.wait_send)

    pl.when(is_early)(finish)
    pl.when(is_first)(add_far)
    pl.when(is_late)(lambda: total_copy(0).wait_recv())
    total = jnp.sum(total_in[...], axis=1, keepdims=True)
    radius = BALL_SCALE * math.sqrt(CHANNELS * ROWS * COLS * fy_count * fx_count)
    factor = jnp.maximum(0.0, 1.0 - DUAL_STEP * radius / jnp.sqrt(total + NORM_EPS))
    factor_ref[...] = jnp.broadcast_to(factor, (1, COLS))

    for z, zs in shares.items():
        pl.when(me_x == z)(functools.partial(hand, zs))
    for z, zs in shares.items():
        pl.when(me_x == z)(functools.partial(arrived, line_in, len(zs), total_sem.at[0]))


def last_step(pa_ref, pb_ref, shifted_ref, factor_ref, image_hbm, dual_hbm, image, dual, sems):
    factor = factor_ref[...]
    copies = []
    for part in range(4):
        for c in range(4 * part, 4 * part + 4):
            image[c] = jnp.maximum(pa_ref[c] - factor * pb_ref[c], 0.0)
            dual[c] = factor * shifted_ref[c]
        chans = pl.ds(4 * part, 4)
        for at, (source, target) in enumerate([(image, image_hbm), (dual, dual_hbm)]):
            copy = pltpu.make_async_copy(source.at[chans], target.at[chans], sems.at[part, at])
            copy.start()
            copies.append(copy)
    for copy in copies:
        copy.wait()


def per_device(fy_count, fx_count, start_image, dirty, sampling, basis_seed, margin):
    forward, backward, column = tables()
    tile = jax.ShapeDtypeStruct((CHANNELS, ROWS, COLS), F32)
    hbm = pl.BlockSpec(memory_space=pltpu.HBM)
    vmem = pl.BlockSpec(memory_space=pltpu.VMEM)
    field = pltpu.VMEM((CHANNELS, ROWS, COLS), F32)
    strips = pltpu.VMEM((GROUPS, ROWS, COLS), F32)
    dma = pltpu.SemaphoreType.DMA

    def body(*refs):
        kernel_body(fy_count, fx_count, *refs)

    pa, pb, shifted, factor = pl.pallas_call(
        body,
        out_shape=(tile, tile, tile, jax.ShapeDtypeStruct((1, COLS), F32)),
        in_specs=[hbm] * 8,
        out_specs=(vmem,) * 4,
        scratch_shapes=[
            field, field, field,
            pltpu.VMEM((RANK, CHANNELS), F32),
            pltpu.SMEM((1, 1, LEVELS, 2), jnp.int32),
            pltpu.VMEM((128, 192), F32), pltpu.VMEM((64, 384), F32), pltpu.VMEM((4 * LEVELS, 256, 256), BF),
            pltpu.VMEM((128, 192), BF), pltpu.VMEM((64, 384), BF),
            strips, field, strips, strips,
            pltpu.VMEM((CHANNELS // 2, 192, 256), BF), pltpu.VMEM((GROUPS, 192, COLS), BF),
            pltpu.VMEM((LEVELS, 64 * PER, 512), BF), pltpu.VMEM((64 * PER, 512), BF),
            pltpu.VMEM((PER // 2, 256, 256), BF), pltpu.VMEM((PER // 4, 256, COLS), BF),
            field, field, pltpu.VMEM((GROUPS, 64, COLS), F32), field, strips, strips,
            pltpu.VMEM((RANK, CHANNELS, COLS), F32),
            pltpu.VMEM((1, COLS), F32), pltpu.VMEM((fx_count, 1, COLS), F32),
            pltpu.VMEM((1, COLS), F32), pltpu.VMEM((fy_count, 1, COLS), F32),
            pltpu.VMEM((1, COLS), F32), pltpu.VMEM((FAR * fy_count, 1, COLS), F32),
            pltpu.VMEM((1, COLS), F32), pltpu.VMEM((1, COLS), F32),
            dma((4, 3)), dma((5,)), dma((HALVES, 3)), dma((HALVES, 3)), dma((3,)), dma((2,)), dma((2,)), dma((2,)), dma((HALVES, 3)), dma((HALVES, 3)),
        ],
        compiler_params=pltpu.CompilerParams(collective_id=0, has_side_effects=True, vmem_limit_bytes=40 * 1024 * 1024),
        name="step",
    )(*(pltpu.with_memory_space_constraint(value, pltpu.HBM) for value in (
        start_image, dirty, sampling, basis_seed.T, margin,
        jnp.asarray(forward, F32), jnp.asarray(backward, F32), jnp.asarray(column, BF))))
    return pl.pallas_call(
        last_step,
        out_shape=(tile, tile),
        in_specs=[vmem] * 4,
        out_specs=(hbm, hbm),
        scratch_shapes=[field, field, dma((4, 2))],
        compiler_params=pltpu.CompilerParams(vmem_limit_bytes=4 * 1024 * 1024),
        name="last",
    )(pa, pb, shifted, factor)


def solution(mesh):
    fy_count, fx_count = mesh.shape["fy"], mesh.shape["fx"]

    def step(*args):
        return per_device(fy_count, fx_count, *args)

    image = P(None, "fy", "fx")
    return jax.shard_map(
        step, mesh=mesh, in_specs=(image, image, image, P(), P("fy", "fx", None, None)),
        out_specs=(image, image), check_vma=False)
```

```python
import functools
import math

import jax
import jax.numpy as jnp
import numpy as np
from jax import lax
from jax.experimental import pallas as pl
from jax.experimental.pallas import tpu as pltpu
from jax.sharding import PartitionSpec as P

MESH = pl.DeviceIdType.MESH
BF = jnp.bfloat16
F32 = jnp.float32

LEVELS = 2
PAD = 32
ROWS = 32
COLS = 128
CHANNELS = 16
RANK = 4
HALVES = 2
EARLY = 5
FIRSTS = ((0, 1), (0, 3), (0, 9), (0, 2), (0, 8), (1, 1), (1, 0))
FAR = 6
PER = CHANNELS // HALVES
GROUPS = CHANNELS // 4


DAUBECHIES = [
    -0.00011747678400228192,
    0.0006754494059985568,
    -0.0003917403729959771,
    -0.00487035299301066,
    0.008746094047015655,
    0.013981027917015516,
    -0.04408825393106472,
    -0.01736930100202211,
    0.128747426620186,
    0.00047248457399797254,
    -0.2840155429624281,
    -0.015829105256023893,
    0.5853546836548691,
    0.6756307362980128,
    0.3128715909144659,
    0.05441584224308161,
]
DUAL_STEP = 0.5
PRIMAL_STEP = 0.5
CLIP_LEVEL = 0.08
BALL_SCALE = 0.8
NORM_EPS = 1e-06


def taps_pair():
    low = [tap / math.sqrt(2.0) for tap in DAUBECHIES]
    high = [(-1.0) ** k * low[len(low) - 1 - k] for k in range(len(low))]
    return low, high


def band_matrix(taps, extent, dilation):
    matrix = np.zeros((extent + PAD, extent), np.float64)
    for k, tap in enumerate(taps):
        for i in range(extent):
            matrix[i + PAD - k * dilation, i] += tap
    return matrix


def split_host(matrix):
    high = matrix.astype(np.float32).astype(jnp.bfloat16)
    low = (matrix - high.astype(np.float64)).astype(np.float32).astype(jnp.bfloat16)
    return high, low


def tables():
    low, high = taps_pair()
    scale = DUAL_STEP / math.sqrt(LEVELS)
    rows, cols = [], []
    for level in range(LEVELS):
        d = 2**level
        rows.append(band_matrix(low, ROWS, d).T)
        rows.append(band_matrix(high, ROWS, d).T)
        both = np.concatenate([band_matrix(low, COLS, d), band_matrix(high, COLS, d)], axis=1) * scale
        cols.append(np.concatenate([both[PAD:]] + [both[:PAD]] * 4, axis=0))
    row_all = np.concatenate(rows, axis=0)
    hi, lo = (part.astype(np.float32) for part in split_host(row_all))
    forward = np.concatenate([hi, hi, lo], axis=1)
    backward = np.concatenate([hi.T, hi.T, lo.T], axis=1)
    column = []
    for level in range(LEVELS):
        column.extend(split_host(cols[level]))
    for level in range(LEVELS):
        column.extend(split_host(cols[level].T))
    return forward, backward, np.stack(column)


def split(value):
    high = value.astype(BF)
    return high, (value - high.astype(F32)).astype(BF)


def dot(a, b):
    return jnp.dot(a, b, preferred_element_type=F32)


def kernel_body(fy_count, fx_count, start_hbm, dirty_hbm, samp_hbm, basis_hbm, margin_hbm, fwd_hbm, bwd_hbm, col_hbm,
                pa_ref, pb_ref, shifted_ref, factor_ref,
                start, dirty, samp, basis, margin, fwd_raw, bwd_raw, col,
                fwd_m, bwd_m, pack, above, left_in, corner_in,
                x_own, x_left, lhs, bands, z_own, z_left, own, up_out, left_out, up_in, left_back, corner_back,
                spec, line_out, line_in, plane_out, plane_in, side_out, direct_in, total_out, total_in,
                input_sem, load_sem, halo_send, halo_recv, line_sem, plane_sem, direct_sem, total_sem, back_send, back_recv):
    me_y, me_x = lax.axis_index("fy"), lax.axis_index("fx")
    below, over = lax.rem(me_y + 1, fy_count), lax.rem(me_y + fy_count - 1, fy_count)
    right, left = lax.rem(me_x + 1, fx_count), lax.rem(me_x + fx_count - 1, fx_count)

    loads = []
    for at, (source, target) in enumerate([(margin_hbm, margin), (basis_hbm, basis), (fwd_hbm, fwd_raw), (bwd_hbm, bwd_raw), (col_hbm, col)]):
        loads.append(pltpu.make_async_copy(source, target, load_sem.at[at]))
    quarters = []
    for part in range(4):
        chans = pl.ds(4 * part, 4)
        quarters.append([])
        for at, (source, target) in enumerate([(start_hbm, start), (dirty_hbm, dirty), (samp_hbm, samp)]):
            copy = pltpu.make_async_copy(source.at[chans], target.at[chans], input_sem.at[part, at])
            copy.start()
            quarters[part].append(copy)

    barrier = pltpu.get_barrier_semaphore()

    def greet(device):
        pl.semaphore_signal(barrier, inc=1, device_id=device, device_id_type=MESH)

    row, chip, core = me_y // 8, lax.rem(me_y // 2, 4), lax.rem(me_y, 2)
    plane = []
    for far in (4, 3, 2, 1, 0):
        for dy in range(4):
            for dx in range(4):
                for dc in range(2):
                    if min(dy, 4 - dy) + min(dx, 4 - dx) == far and (dy, dx, dc) != (0, 0, 0):
                        at = 8 * lax.rem(row + dy, 4) + 2 * lax.rem(chip + dx, 4) + lax.rem(core + dc, 2)
                        plane.append({"fy": at, "fx": me_x})
    line = {}
    for k in range(1, fx_count):
        line[k] = {"fy": me_y, "fx": lax.rem(me_x + k, fx_count)}
    order = sorted(line, key=lambda k: -min(k, fx_count - k))
    is_early, is_late = me_x < EARLY, me_x >= EARLY
    has_left, has_right = me_x > 0, me_x < fx_count - 1
    has_above, has_below = me_y > 0, me_y < fy_count - 1
    up_left, down_right = jnp.logical_and(has_above, has_left), jnp.logical_and(has_below, has_right)

    far0 = fx_count // 2 - 2
    is_far = jnp.logical_and(me_x >= far0, me_x < far0 + FAR)
    is_first = functools.reduce(jnp.logical_or, [jnp.logical_and(me_x == z, me_y == y) for z, y in FIRSTS])

    def greet_far():
        for z in range(far0, far0 + FAR):
            def each(k, carry, z=z):
                greet({"fy": lax.rem(me_y + k, fy_count), "fx": z})
                return carry

            lax.fori_loop(1, fy_count, each, 0)

    def greet_many():
        for k in order:
            greet(line[k])
        for device in plane:
            greet(device)

    def greet_few():
        pl.when(has_above)(lambda: greet({"fy": over, "fx": me_x}))
        pl.when(has_below)(lambda: greet({"fy": below, "fx": me_x}))
        greet({"fy": me_y, "fx": left})

    pl.when(is_early)(greet_many)
    pl.when(is_first)(greet_far)
    pl.when(is_late)(greet_few)
    pl.when(jnp.logical_and(is_late, has_right))(lambda: greet({"fy": me_y, "fx": right}))
    pl.when(down_right)(lambda: greet({"fy": below, "fx": right}))
    pl.when(up_left)(lambda: greet({"fy": over, "fx": left}))

    lane = lax.broadcasted_iota(jnp.int32, (1, COLS), 1)
    block = lane // PAD

    energy = jnp.zeros((ROWS, COLS), F32)
    for c in range(CHANNELS):
        if c % 4 == 0:
            for copy in quarters[c // 4]:
                copy.wait()
        value = DUAL_STEP * samp[c] * start[c] - DUAL_STEP * dirty[c]
        shifted_ref[c] = value
        energy = energy + value * value
    energy = jnp.sum(energy, axis=0, keepdims=True)
    line_out[...] = energy

    one = lambda flag: flag.astype(jnp.int32)
    guests = jnp.where(
        is_early,
        len(plane) + EARLY - 1 + one(me_x == EARLY - 1),
        one(has_above) + one(has_below) + EARLY + one(me_x > EARLY) + one(has_right)
        + one(is_far) * sum(one(me_y != y) for z, y in FIRSTS)) + one(up_left) + one(down_right)
    pl.semaphore_wait(barrier, guests)

    def line_copy(z):
        return pltpu.make_async_remote_copy(
            src_ref=line_out, dst_ref=line_in.at[me_x], send_sem=line_sem.at[0], recv_sem=line_sem.at[1 + one(is_far)],
            device_id={"fy": me_y, "fx": z}, device_id_type=MESH)

    directs = []
    for z, y in FIRSTS:
        directs.append(pltpu.make_async_remote_copy(
            src_ref=line_out, dst_ref=direct_in.at[lax.rem(me_x, FAR) * fy_count + me_y], send_sem=direct_sem.at[0],
            recv_sem=direct_sem.at[1 + lax.rem(me_x, FAR)], device_id={"fy": y, "fx": z}, device_id_type=MESH))

    def send_direct():
        for copy in directs:
            copy.start()

    pl.when(is_far)(send_direct)
    for z in range(EARLY):
        pl.when(me_x != z)(lambda z=z: line_copy(z).start())

    for copy in loads:
        copy.start()
    for g in range(GROUPS):
        total = jnp.zeros((ROWS, COLS), F32)
        for q in range(4):
            value = start[4 * g + q]
            moved = value if q == 3 else pltpu.roll(value, PAD * (q + 1), 1)
            total = jnp.where(block == q, moved, total)
        pack[g] = total

    halos = []
    for h in range(HALVES):
        chans = pl.ds(h * PER, PER)
        groups = pl.ds(h * PER // 4, PER // 4)
        for at, (source, target, device) in enumerate([
            (start.at[chans], above.at[chans], {"fy": below, "fx": me_x}),
            (pack.at[groups], left_in.at[groups], {"fy": me_y, "fx": right}),
            (pack.at[groups], corner_in.at[groups], {"fy": below, "fx": right}),
        ]):
            copy = pltpu.make_async_remote_copy(
                src_ref=source, dst_ref=target, send_sem=halo_send.at[h, at], recv_sem=halo_recv.at[h, at],
                device_id=device, device_id_type=MESH)
            pl.when((has_below, has_right, down_right)[at])(copy.start)
            halos.append(copy)

    def clear(*refs):
        for ref in refs:
            ref[...] = jnp.zeros_like(ref)

    pl.when(jnp.logical_not(has_above))(functools.partial(clear, above))
    pl.when(jnp.logical_not(has_left))(functools.partial(clear, left_in))
    pl.when(jnp.logical_not(up_left))(functools.partial(clear, corner_in))
    pl.when(jnp.logical_not(has_below))(functools.partial(clear, up_in))
    pl.when(jnp.logical_not(has_right))(functools.partial(clear, left_back))
    pl.when(jnp.logical_not(down_right))(functools.partial(clear, corner_back))

    for copy in loads:
        copy.wait()
    row_has = (me_y > 0).astype(jnp.int32)
    col_has = (me_x > 0).astype(jnp.int32)
    keep_rows = [margin[0, 0, l, 0] * row_has for l in range(LEVELS)]
    keep_cols = [margin[0, 0, l, 1] * col_has for l in range(LEVELS)]

    row_at = lax.broadcasted_iota(jnp.int32, (128, 192), 0)
    col_at = lax.rem(lax.broadcasted_iota(jnp.int32, (128, 192), 1), 64)
    reach = jnp.where(row_at < 64, keep_rows[0], keep_rows[1])
    fwd_m[...] = jnp.where(PAD - col_at <= reach, fwd_raw[...], 0.0).astype(BF)
    row_at = lax.broadcasted_iota(jnp.int32, (64, 384), 0)
    col_at = lax.rem(lax.broadcasted_iota(jnp.int32, (64, 384), 1), 128)
    reach = jnp.where(col_at < 64, keep_rows[0], keep_rows[1])
    bwd_m[...] = jnp.where(PAD - row_at <= reach, bwd_raw[...], 0.0).astype(BF)

    kept = []
    for l in range(LEVELS):
        inside = PAD - lax.rem(lane, PAD) <= keep_cols[l]
        kept.append([jnp.logical_and(inside, block == q) for q in range(4)])

    columns = []
    diagonal = lax.broadcasted_iota(jnp.int32, (CHANNELS, CHANNELS), 0) == lax.broadcasted_iota(jnp.int32, (CHANNELS, CHANNELS), 1)
    for r in range(RANK):
        vector = jnp.sum(jnp.where(diagonal, basis[r : r + 1, :], 0.0), axis=1, keepdims=True)
        vector = jnp.broadcast_to(vector, (CHANNELS, COLS))
        for previous in columns:
            vector = vector - jnp.sum(previous * vector, axis=0, keepdims=True) * previous
        vector = vector / jnp.sqrt(jnp.sum(vector * vector, axis=0, keepdims=True))
        columns.append(vector)
        spec[r] = vector

    def project(field):
        weights = []
        for r in range(RANK):
            total = spec[r, 0:1, :] * field(0)
            for c in range(1, CHANNELS):
                total = total + spec[r, c : c + 1, :] * field(c)
            weights.append(total)

        def channel(c):
            total = spec[0, c : c + 1, :] * weights[0]
            for r in range(1, RANK):
                total = total + spec[r, c : c + 1, :] * weights[r]
            return total

        return channel

    pb = project(lambda c: PRIMAL_STEP * samp[c] * shifted_ref[c])
    for c in range(CHANNELS):
        pb_ref[c] = pb(c)

    def place(target, p, part, row0, value):
        high, low = split(value)
        lanes = pl.ds(COLS * part, COLS)
        target[p, pl.ds(row0, ROWS), lanes] = high
        target[p, pl.ds(64 + row0, ROWS), lanes] = low
        target[p, pl.ds(128 + row0, ROWS), lanes] = high

    for c in range(CHANNELS):
        place(x_own, c // 2, c % 2, PAD, start[c])

    backs = []
    for h in range(HALVES):
        for flag, copy in zip((has_above, has_left, up_left), halos[3 * h : 3 * h + 3]):
            pl.when(flag)(copy.wait_recv)
        first = h * PER
        for c in range(first, first + PER):
            place(x_own, c // 2, c % 2, 0, above[c])
        for g in range(first // 4, (first + PER) // 4):
            place(x_left, g, 0, 0, corner_in[g])
            place(x_left, g, 0, PAD, left_in[g])
        for p in range(first // 2, (first + PER) // 2):
            u = dot(fwd_m[...], x_own[p])
            high, low = split(u)
            for part in range(2):
                c = 2 * p + part - first
                lanes = slice(COLS * part, COLS * (part + 1))
                for l in range(LEVELS):
                    lhs[l, pl.ds(64 * c, 64), 0:128] = high[64 * l : 64 * l + 64, lanes]
                    lhs[l, pl.ds(64 * c, 64), 256:384] = low[64 * l : 64 * l + 64, lanes]
        for g in range(first // 4, (first + PER) // 4):
            u = dot(fwd_m[...], x_left[g])
            for q in range(4):
                c = 4 * g + q - first
                for l in range(LEVELS):
                    high, low = split(jnp.where(kept[l][q], u[64 * l : 64 * l + 64, :], 0.0))
                    lhs[l, pl.ds(64 * c, 64), 128:256] = high
                    lhs[l, pl.ds(64 * c, 64), 384:512] = low
        z_sum = [[jnp.zeros((64, COLS), F32) for l in range(LEVELS)] for g in range(PER // 4)]
        for l in range(LEVELS):
            acc = dot(lhs[l, :, 0:256], col[2 * l]) + dot(lhs[l, :, 256:512], col[2 * l]) + dot(lhs[l, :, 0:256], col[2 * l + 1])
            acc = jnp.clip(acc, -CLIP_LEVEL, CLIP_LEVEL)
            high, low = split(acc)
            for c in range(PER):
                zero = jnp.zeros((32, COLS), BF)
                top, mid, end = 64 * c, 64 * c + 32, 64 * c + 64
                bands[pl.ds(top, 32), 0:128] = zero
                bands[pl.ds(top, 32), 256:384] = zero
                bands[pl.ds(top, 32), 128:256] = high[top:mid, 128:256]
                bands[pl.ds(top, 32), 384:512] = low[top:mid, 128:256]
                bands[pl.ds(mid, 32), 0:256] = high[mid:end, :]
                bands[pl.ds(mid, 32), 256:512] = low[mid:end, :]
            at = 2 * LEVELS + 2 * l
            z = dot(bands[:, 0:256], col[at]) + dot(bands[:, 256:512], col[at]) + dot(bands[:, 0:256], col[at + 1])
            for c in range(PER):
                high, low = split(z[64 * c : 64 * c + 64, 0:128])
                lanes = pl.ds(COLS * (c % 2), COLS)
                z_own[c // 2, pl.ds(64 * l, 64), lanes] = high
                z_own[c // 2, pl.ds(128 + 64 * l, 64), lanes] = low
                piece = z[64 * c : 64 * c + 64, 128:256]
                z_sum[c // 4][l] = z_sum[c // 4][l] + jnp.where(kept[l][c % 4], piece, 0.0)
        for g in range(PER // 4):
            for l in range(LEVELS):
                high, low = split(z_sum[g][l])
                z_left[g, pl.ds(64 * l, 64), :] = high
                z_left[g, pl.ds(128 + 64 * l, 64), :] = low
            left_out[first // 4 + g] = dot(bwd_m[:, 0:256], z_left[g]) + dot(bwd_m[:, 256:384], z_left[g, 0:128, :])
        for p in range(PER // 2):
            r = dot(bwd_m[:, 0:256], z_own[p]) + dot(bwd_m[:, 256:384], z_own[p, 0:128, :])
            for part in range(2):
                c = first + 2 * p + part
                up_out[c] = r[0:32, COLS * part : COLS * (part + 1)]
                own[c] = r[32:64, COLS * part : COLS * (part + 1)]
        chans = pl.ds(first, PER)
        groups = pl.ds(first // 4, PER // 4)
        for at, (source, target, device) in enumerate([
            (left_out.at[groups, pl.ds(32, 32), :], left_back.at[groups], {"fy": me_y, "fx": left}),
            (left_out.at[groups, pl.ds(0, 32), :], corner_back.at[groups], {"fy": over, "fx": left}),
            (up_out.at[chans], up_in.at[chans], {"fy": over, "fx": me_x}),
        ]):
            copy = pltpu.make_async_remote_copy(
                src_ref=source, dst_ref=target, send_sem=back_send.at[h, at], recv_sem=back_recv.at[h, at],
                device_id=device, device_id_type=MESH)
            pl.when((has_left, up_left, has_above)[at])(copy.start)
            backs.append(copy)

    def arrived(ref, count, sem):
        pltpu.make_async_copy(ref.at[pl.ds(0, count)], ref.at[pl.ds(0, count)], sem).wait()

    def plane_copy(source, device):
        return pltpu.make_async_remote_copy(
            src_ref=source, dst_ref=plane_in.at[me_y], send_sem=plane_sem.at[0], recv_sem=plane_sem.at[1],
            device_id=device, device_id_type=MESH)

    def exchange():
        arrived(line_in, fx_count - 1 - FAR, line_sem.at[1])
        line_in[me_x] = line_out[...]
        side = jnp.sum(line_in[0:far0], axis=0) + jnp.sum(line_in[far0 + FAR :], axis=0)
        side_out[...] = side
        plane_in[me_y] = side
        for z, y in FIRSTS:
            pl.when(jnp.logical_and(me_x == z, me_y != y))(plane_copy(side_out, {"fy": y, "fx": z}).start)
        arrived(line_in, FAR, line_sem.at[2])
        whole = side_out[...] + jnp.sum(line_in[far0 : far0 + FAR], axis=0)
        plane_out[...] = whole

        def keep_whole():
            plane_in[me_y] = whole

        pl.when(jnp.logical_not(is_first))(keep_whole)

        def send_whole(skip):
            for y in sorted(range(fy_count), key=lambda y: min(y // 8, 4 - y // 8) + min(y // 2 % 4, 4 - y // 2 % 4)):
                if y not in skip:
                    pl.when(me_y != y)(plane_copy(plane_out, {"fy": y, "fx": me_x}).start)

        special = sorted({z for z, y in FIRSTS})
        for at in special:
            pl.when(me_x == at)(functools.partial(send_whole, [y for z, y in FIRSTS if z == at]))
        pl.when(me_x > special[-1])(functools.partial(send_whole, []))

    pl.when(is_early)(exchange)

    for at, copy in enumerate(backs):
        pl.when((has_right, down_right, has_below)[at % 3])(copy.wait_recv)
    for g in range(GROUPS):
        strip = left_back[g] + corner_back[g]
        for q in range(4):
            c = 4 * g + q
            moved = strip if q == 3 else pltpu.roll(strip, COLS - PAD * (q + 1), 1)
            own[c] = start[c] - (own[c] + up_in[c] + jnp.where(block == 3, moved, 0.0))
    pa = project(lambda c: own[c])
    for c in range(CHANNELS):
        pa_ref[c] = pa(c)

    def total_copy(z):
        return pltpu.make_async_remote_copy(
            src_ref=total_out, dst_ref=total_in, send_sem=total_sem.at[0], recv_sem=total_sem.at[1],
            device_id={"fy": me_y, "fx": z}, device_id_type=MESH)

    middle = (2 * EARLY + fx_count - 5) // 2
    shares = {EARLY - 2: range(middle + 1, fx_count), EARLY - 1: range(middle, EARLY - 1, -1)}

    def finish():
        arrived(plane_in, fy_count - 1, plane_sem.at[1])
        total = jnp.sum(plane_in[...], axis=0)
        total_in[...] = total
        total_out[...] = total

    def add_far():
        total = total_in[...]
        for z in sorted(range(far0, far0 + FAR), key=lambda z: -abs(z - far0 - 2.4)):
            at = z % FAR
            arrived(direct_in, fy_count, direct_sem.at[1 + at])
            total = total + jnp.sum(direct_in[at * fy_count : (at + 1) * fy_count], axis=0)
        total_in[...] = total

    def hand(zs):
        for z in zs:
            total_copy(z).start()

    for at, copy in enumerate(halos):
        pl.when((has_below, has_right, down_right)[at % 3])(copy.wait_send)
    for at, copy in enumerate(backs):
        pl.when((has_left, up_left, has_above)[at % 3])(copy.wait_send)

    def early_sent():
        arrived(line_in, EARLY - 1, line_sem.at[0])
        arrived(plane_in, fy_count - 1, plane_sem.at[0])

    pl.when(is_early)(early_sent)
    pl.when(is_late)(lambda: arrived(line_in, EARLY, line_sem.at[0]))
    pl.when(is_far)(lambda: arrived(line_in, len(FIRSTS), direct_sem.at[0]))

    pl.when(is_early)(finish)
    pl.when(is_first)(add_far)
    pl.when(is_late)(lambda: total_copy(0).wait_recv())
    total = jnp.sum(total_in[...], axis=1, keepdims=True)
    radius = BALL_SCALE * math.sqrt(CHANNELS * ROWS * COLS * fy_count * fx_count)
    factor = jnp.maximum(0.0, 1.0 - DUAL_STEP * radius / jnp.sqrt(total + NORM_EPS))
    factor_ref[...] = jnp.broadcast_to(factor, (1, COLS))

    for z, zs in shares.items():
        pl.when(me_x == z)(functools.partial(hand, zs))
    for z, zs in shares.items():
        pl.when(me_x == z)(functools.partial(arrived, line_in, len(zs), total_sem.at[0]))


def last_step(pa_ref, pb_ref, shifted_ref, factor_ref, image_hbm, dual_hbm, image, dual, sems):
    factor = factor_ref[...]
    copies = []
    for part in range(4):
        for c in range(4 * part, 4 * part + 4):
            image[c] = jnp.maximum(pa_ref[c] - factor * pb_ref[c], 0.0)
            dual[c] = factor * shifted_ref[c]
        chans = pl.ds(4 * part, 4)
        for at, (source, target) in enumerate([(image, image_hbm), (dual, dual_hbm)]):
            copy = pltpu.make_async_copy(source.at[chans], target.at[chans], sems.at[part, at])
            copy.start()
            copies.append(copy)
    for copy in copies:
        copy.wait()


def per_device(fy_count, fx_count, start_image, dirty, sampling, basis_seed, margin):
    forward, backward, column = tables()
    tile = jax.ShapeDtypeStruct((CHANNELS, ROWS, COLS), F32)
    hbm = pl.BlockSpec(memory_space=pltpu.HBM)
    vmem = pl.BlockSpec(memory_space=pltpu.VMEM)
    field = pltpu.VMEM((CHANNELS, ROWS, COLS), F32)
    strips = pltpu.VMEM((GROUPS, ROWS, COLS), F32)
    dma = pltpu.SemaphoreType.DMA

    def body(*refs):
        kernel_body(fy_count, fx_count, *refs)

    pa, pb, shifted, factor = pl.pallas_call(
        body,
        out_shape=(tile, tile, tile, jax.ShapeDtypeStruct((1, COLS), F32)),
        in_specs=[hbm] * 8,
        out_specs=(vmem,) * 4,
        scratch_shapes=[
            field, field, field,
            pltpu.VMEM((RANK, CHANNELS), F32),
            pltpu.SMEM((1, 1, LEVELS, 2), jnp.int32),
            pltpu.VMEM((128, 192), F32), pltpu.VMEM((64, 384), F32), pltpu.VMEM((4 * LEVELS, 256, 256), BF),
            pltpu.VMEM((128, 192), BF), pltpu.VMEM((64, 384), BF),
            strips, field, strips, strips,
            pltpu.VMEM((CHANNELS // 2, 192, 256), BF), pltpu.VMEM((GROUPS, 192, COLS), BF),
            pltpu.VMEM((LEVELS, 64 * PER, 512), BF), pltpu.VMEM((64 * PER, 512), BF),
            pltpu.VMEM((PER // 2, 256, 256), BF), pltpu.VMEM((PER // 4, 256, COLS), BF),
            field, field, pltpu.VMEM((GROUPS, 64, COLS), F32), field, strips, strips,
            pltpu.VMEM((RANK, CHANNELS, COLS), F32),
            pltpu.VMEM((1, COLS), F32), pltpu.VMEM((fx_count, 1, COLS), F32),
            pltpu.VMEM((1, COLS), F32), pltpu.VMEM((fy_count, 1, COLS), F32),
            pltpu.VMEM((1, COLS), F32), pltpu.VMEM((FAR * fy_count, 1, COLS), F32),
            pltpu.VMEM((1, COLS), F32), pltpu.VMEM((1, COLS), F32),
            dma((4, 3)), dma((5,)), dma((HALVES, 3)), dma((HALVES, 3)), dma((3,)), dma((2,)), dma((1 + FAR,)), dma((2,)), dma((HALVES, 3)), dma((HALVES, 3)),
        ],
        compiler_params=pltpu.CompilerParams(collective_id=0, has_side_effects=True, vmem_limit_bytes=40 * 1024 * 1024),
        name="step",
    )(*(pltpu.with_memory_space_constraint(value, pltpu.HBM) for value in (
        start_image, dirty, sampling, basis_seed.T, margin,
        jnp.asarray(forward, F32), jnp.asarray(backward, F32), jnp.asarray(column, BF))))
    return pl.pallas_call(
        last_step,
        out_shape=(tile, tile),
        in_specs=[vmem] * 4,
        out_specs=(hbm, hbm),
        scratch_shapes=[field, field, dma((4, 2))],
        compiler_params=pltpu.CompilerParams(vmem_limit_bytes=4 * 1024 * 1024),
        name="last",
    )(pa, pb, shifted, factor)


def solution(mesh):
    fy_count, fx_count = mesh.shape["fy"], mesh.shape["fx"]

    def step(*args):
        return per_device(fy_count, fx_count, *args)

    image = P(None, "fy", "fx")
    return jax.shard_map(
        step, mesh=mesh, in_specs=(image, image, image, P(), P("fy", "fx", None, None)),
        out_specs=(image, image), check_vma=False)
```
